32 devices in a mesh: blocks: 8 (over z, core), lev: 4 (over y, x).
Axes of the slice: x: 2, y: 2, z: 4, core: 2. Of those that a mesh axis runs over, the one named last changes fastest.
Arguments:
- tracers: float32 [8, 4, 8, 128, 128], P('blocks', 'lev'), may hold values from -6 to 6
- east_velocity: float32 [8, 8, 128, 128], P('blocks'), may hold values from -0.24 to 0.24
- north_velocity: float32 [8, 8, 128, 128], P('blocks'), may hold values from -0.24 to 0.24
- upward_velocity: float32 [8, 8, 128, 128], P('blocks'), may hold values from -0.24 to 0.24
- target: float32 [8, 4, 8, 128, 128], P('blocks', 'lev'), may hold values from 0.09375 to 12.65625
- bottom: int32 [8, 128, 128], P('blocks'), may hold values from 0 to 8, as said below
- shave_fraction: float32 [8, 128, 128], P('blocks'), may hold values from 0.05 to 1, as said below
- side_bottom: int32 [8, 4, 128], P('blocks'), may hold values from 0 to 8, as said below
- neighbors: int32 [8, 4], P('blocks'), may hold values from -1 to 7, as said below
- fold_partner: int32 [8], P('blocks'), may hold values from -1 to 7, as said below
- thin_pairs: int32 [8, 2, 128], P('blocks'), may hold values from 0 to 16383, as said below
Outputs:
- new_tracers: float32 [8, 4, 8, 128, 128], P('blocks', 'lev')
The draws below stay inside these ranges and needn't reach their ends.
Inputs may be any that keep to these rules, and one draw needn't show every extreme that they name: The blocks form a grid of 3 block columns, periodic from west to east, and 4 block rows; entries are mutual: neighbors[b,0] = c exactly when neighbors[c,1] = b, and neighbors[b,2] = c exactly when neighbors[c,3] = b; a block's entries that are not -1 differ; blocks of the top row have -1 to the north. `fold_partner`: set exactly for the blocks of the top row; mutual, a block may be its own partner. `bottom`: every block has wet columns. `side_bottom`: equals the bottom of the adjacent column or row of the neighbouring block, across the north fold the partner's top row in reversed order, 0 where no block lies. `thin_pairs`: thin cells of a block are distinct and have bottom 1 or more; each partner is the cell just east of its thin cell in the same row, with a bottom no smaller; no cell appears twice in a block. `shave_fraction`: listed thin cells have 0.05 to 0.2, all other cells 0.5 to 1.
All inputs are finite; a program needn't handle non-finite values.
Results may differ from the reference program's by a relative error of at most 0.0003.
Values sent between devices are 32-bit elements; how exact they have to be, the bound alone decides.
A program may use at most 64 MiB of HBM per device.

```python
import math
import jax
import jax.numpy as jnp
from jax import lax

BS = 128
LEVELS = 8
NTHIN = 128
TRACERS = 4
GX = 3
GY = 4
N_BLOCKS = 8


def block_layout(key):
    layout_key = jax.random.fold_in(key, 11)
    inner = (GY - 1) * GX
    chosen = jax.random.permutation(jax.random.fold_in(layout_key, 1), inner)[:N_BLOCKS - GX]
    tiles = jnp.concatenate([chosen.astype(jnp.int32), inner + jnp.arange(GX, dtype=jnp.int32)])
    ordering = jax.random.permutation(jax.random.fold_in(layout_key, 2), N_BLOCKS)
    tile_of = tiles[ordering]
    block_of = jnp.full((GX * GY,), -1, jnp.int32).at[tile_of].set(jnp.arange(N_BLOCKS, dtype=jnp.int32))
    column = tile_of % GX
    row_index = tile_of // GX
    west = block_of[row_index * GX + (column + GX - 1) % GX]
    east = block_of[row_index * GX + (column + 1) % GX]
    south = jnp.where(row_index > 0, block_of[jnp.maximum(row_index - 1, 0) * GX + column], -1)
    north = jnp.where(row_index < GY - 1, block_of[jnp.minimum(row_index + 1, GY - 1) * GX + column], -1)
    mirror = jnp.where(row_index == GY - 1, block_of[row_index * GX + GX - 1 - column], -1)
    return (jnp.stack([west, east, south, north], 1).astype(jnp.int32), mirror.astype(jnp.int32))


def column_draw(key):
    column_key = jax.random.fold_in(key, 23)

    def one_block(index):
        block_key = jax.random.fold_in(column_key, index)
        threshold = jax.random.randint(jax.random.fold_in(block_key, 4), (), 1, 13)
        landing = jax.random.randint(jax.random.fold_in(block_key, 1), (BS * BS,), 0, 20) < threshold
        depth_draw = jax.random.randint(jax.random.fold_in(block_key, 2), (BS * BS,), 1, LEVELS + 1)
        levels_wet = jnp.where(landing, 0, depth_draw).astype(jnp.int32)
        thin_cells = (2 * jax.random.permutation(jax.random.fold_in(block_key, 3), BS * BS // 2)[:NTHIN]).astype(jnp.int32)
        partner = thin_cells + 1
        levels_wet = levels_wet.at[thin_cells].set(jnp.maximum(levels_wet[thin_cells], 1))
        levels_wet = levels_wet.at[partner].set(jnp.maximum(levels_wet[partner], levels_wet[thin_cells]))
        return (levels_wet, jnp.stack([thin_cells, partner]))
    return jax.vmap(one_block)(jnp.arange(N_BLOCKS, dtype=jnp.int32))


def draw_neighbors(key, part):
    return block_layout(key)[0]


def draw_fold_partner(key, part):
    return block_layout(key)[1]


def draw_bottom(key, part):
    return column_draw(key)[0].reshape(N_BLOCKS, BS, BS)


def draw_thin_pairs(key, part):
    return column_draw(key)[1]


def take_rows(edge, index):
    safe = jnp.maximum(index, 0)
    return jnp.where((index >= 0)[:, None], edge[safe], 0)


def draw_side_bottom(key, part):
    sides, mirror = block_layout(key)
    grid = column_draw(key)[0].reshape(N_BLOCKS, BS, BS)
    west = take_rows(grid[:, :, BS - 1], sides[:, 0])
    east = take_rows(grid[:, :, 0], sides[:, 1])
    south = take_rows(grid[:, BS - 1, :], sides[:, 2])
    north = take_rows(grid[:, 0, :], sides[:, 3]) + take_rows(grid[:, BS - 1, ::-1], mirror)
    return jnp.stack([west, east, south, north], 1).astype(jnp.int32)


def draw_shave_fraction(key, part):
    pairs = column_draw(key)[1]
    full_shape = (N_BLOCKS, BS * BS)
    unit_first = jax.random.uniform(jax.random.fold_in(key, 41), full_shape, jnp.float32)
    unit_second = jax.random.uniform(jax.random.fold_in(key, 42), full_shape, jnp.float32)
    regular = 0.5 + 0.5 * unit_first
    thin_value = 0.05 + 0.15 * unit_second
    marks = jnp.zeros(full_shape, jnp.int32).at[jnp.arange(N_BLOCKS)[:, None], pairs[:, 0]].set(1)
    return jnp.where(marks == 1, thin_value, regular).reshape(N_BLOCKS, BS, BS)


def draw_target(key, part):
    block_ramp = 0.5 + jnp.arange(N_BLOCKS, dtype=jnp.float32) / (N_BLOCKS - 1)
    tracer_ramp = 0.5 + jnp.arange(TRACERS, dtype=jnp.float32) / (TRACERS - 1)
    full_shape = (N_BLOCKS, TRACERS, LEVELS, BS, BS)
    block_unit = jax.random.uniform(jax.random.fold_in(key, 61), (N_BLOCKS,), jnp.float32)
    level_unit = jax.random.uniform(jax.random.fold_in(key, 62), (TRACERS, LEVELS), jnp.float32)
    cell_unit = jax.random.uniform(jax.random.fold_in(key, 63), full_shape, jnp.float32)
    block_scale = jnp.exp(math.log(3.0) * block_unit)
    level_scale = 0.75 + 0.5 * level_unit
    cell_scale = 0.5 + cell_unit
    outer = (block_ramp * block_scale)[:, None, None, None, None] * tracer_ramp[None, :, None, None, None]
    return outer * level_scale[None, :, :, None, None] * cell_scale


def steps_of(stream_key, extent, split, smallest, top_value):
    gain = 1.0
    for position, parts in split:
        heights = jax.random.uniform(jax.random.fold_in(jax.random.fold_in(stream_key, 6), position), (parts,), jnp.float32, smallest / len(split), top_value / len(split))
        gain = gain * jnp.repeat(jnp.exp(heights), extent[position] // parts).reshape((-1,) + (1,) * (len(extent) - 1 - position))
    return gain


def normal_values(key, dims, scale, limit, shards=(), held_as=jnp.bfloat16):
    array = jax.random.normal(key, dims, jnp.float32) * scale
    if len(shards) > 0:
        array = steps_of(key, dims, shards, -0.22, 0.18) * array
    return jnp.clip(array, min=-limit, max=limit).astype(held_as)


def setup_inputs(seed: int = 0) -> dict:
    key_list = jax.random.split(jax.random.key(seed), 12)
    return {
        "tracers": normal_values(key_list[0], (N_BLOCKS, TRACERS, LEVELS, BS, BS), 1.0, 6.0, ((0, 8), (1, 4)), jnp.float32),
        "east_velocity": jnp.clip(jax.random.uniform(key_list[1], (N_BLOCKS, LEVELS, BS, BS), jnp.float32, -0.24, 0.24) * steps_of(key_list[1], (N_BLOCKS, LEVELS, BS, BS), ((0, 8),), -0.4, 0.0), -0.24, 0.24),
        "north_velocity": jnp.clip(jax.random.uniform(key_list[2], (N_BLOCKS, LEVELS, BS, BS), jnp.float32, -0.24, 0.24) * steps_of(key_list[2], (N_BLOCKS, LEVELS, BS, BS), ((0, 8),), -0.4, 0.0), -0.24, 0.24),
        "upward_velocity": jnp.clip(jax.random.uniform(key_list[3], (N_BLOCKS, LEVELS, BS, BS), jnp.float32, -0.24, 0.24) * steps_of(key_list[3], (N_BLOCKS, LEVELS, BS, BS), ((0, 8),), -0.4, 0.0), -0.24, 0.24),
        "target": draw_target(jax.random.fold_in(key_list[11], 71), 0),
        "bottom": draw_bottom(jax.random.fold_in(key_list[11], 71), 0),
        "shave_fraction": draw_shave_fraction(jax.random.fold_in(key_list[11], 71), 0),
        "side_bottom": draw_side_bottom(jax.random.fold_in(key_list[11], 71), 0),
        "neighbors": draw_neighbors(jax.random.fold_in(key_list[11], 71), 0),
        "fold_partner": draw_fold_partner(jax.random.fold_in(key_list[11], 71), 0),
        "thin_pairs": draw_thin_pairs(jax.random.fold_in(key_list[11], 71), 0),
    }


RATE = 0.5


def upwind(face, first, second):
    return jnp.maximum(face, 0.0) * first + jnp.minimum(face, 0.0) * second


def column_masks(levels, bottom, shave_fraction):
    level_grid = levels[None, None, :, None, None]
    column_bottom = bottom[:, None, None]
    wet = level_grid < column_bottom
    thick = jnp.where(level_grid < column_bottom - 1, 1.0, jnp.where(level_grid == column_bottom - 1, shave_fraction[:, None, None], 0.0))
    return wet, thick


def level_pair(field):
    zero_level = jnp.zeros_like(field[:, :, :1])
    return jnp.concatenate([zero_level, field[:, :, :-1]], 2), jnp.concatenate([field[:, :, 1:], zero_level], 2)


def advected_field(tracers, east_flow, north_flow, upward_flow, levels, bottom, wet, thick, side_bottom, west_pair, east_pair, south_pair, north_pair):
    level_grid = levels[None, None, :, None, None]
    column_bottom = bottom[:, None, None]
    edge_levels = levels[None, None, :, None]
    wet_west = edge_levels < side_bottom[:, 0][:, None, None, :]
    wet_east = edge_levels < side_bottom[:, 1][:, None, None, :]
    wet_south = edge_levels < side_bottom[:, 2][:, None, None, :]
    wet_north = edge_levels < side_bottom[:, 3][:, None, None, :]
    east_values = jnp.concatenate([tracers[..., 1:], east_pair[0][..., None]], -1)
    east_flows = jnp.concatenate([east_flow[..., 1:], east_pair[1][..., None]], -1)
    east_wets = jnp.concatenate([wet[..., 1:], wet_east[..., None]], -1)
    flux_east = upwind(jnp.where(wet & east_wets, 0.5 * (east_flow + east_flows), 0.0), tracers, east_values)
    west_face = jnp.where(wet_west & wet[..., 0], 0.5 * (west_pair[1] + east_flow[..., 0]), 0.0)
    flux_west = jnp.concatenate([upwind(west_face, west_pair[0], tracers[..., 0])[..., None], flux_east[..., :-1]], -1)
    north_values = jnp.concatenate([tracers[..., 1:, :], north_pair[0][..., None, :]], -2)
    north_flows = jnp.concatenate([north_flow[..., 1:, :], north_pair[1][..., None, :]], -2)
    north_wets = jnp.concatenate([wet[..., 1:, :], wet_north[..., None, :]], -2)
    flux_north = upwind(jnp.where(wet & north_wets, 0.5 * (north_flow + north_flows), 0.0), tracers, north_values)
    south_face = jnp.where(wet_south & wet[..., 0, :], 0.5 * (south_pair[1] + north_flow[..., 0, :]), 0.0)
    flux_south = jnp.concatenate([upwind(south_face, south_pair[0], tracers[..., 0, :])[..., None, :], flux_north[..., :-1, :]], -2)
    above_values, below_values = level_pair(tracers)
    above_flow, below_flow = level_pair(upward_flow)
    wet_above = (level_grid >= 1) & (level_grid - 1 < column_bottom)
    wet_below = level_grid + 1 < column_bottom
    flux_lower = upwind(jnp.where(wet & wet_below, 0.5 * (upward_flow + below_flow), 0.0), below_values, tracers)
    flux_upper = upwind(jnp.where(wet & wet_above, 0.5 * (above_flow + upward_flow), 0.0), tracers, above_values)
    divergence = flux_west - flux_east + flux_south - flux_north + flux_lower - flux_upper
    return tracers + jnp.where(wet, divergence / jnp.where(wet, thick, 1.0), 0.0)


def merge_block(field, bottom, shave_fraction, pairs, levels):
    flat = field.reshape(field.shape[0], field.shape[1], -1)
    thin_cells = pairs[0]
    partner = pairs[1]
    depth_index = bottom[thin_cells] - 1
    thin_thick = shave_fraction[thin_cells]
    partner_thick = jnp.where(bottom[partner] - 1 == depth_index, shave_fraction[partner], 1.0)
    thin_values = flat[:, :, thin_cells]
    partner_values = flat[:, :, partner]
    merged = (thin_thick * thin_values + partner_thick * partner_values) / (thin_thick + partner_thick)
    struck = levels[:, None] == depth_index[None, :]
    flat = flat.at[:, :, thin_cells].set(jnp.where(struck, merged, thin_values))
    flat = flat.at[:, :, partner].set(jnp.where(struck, merged, partner_values))
    return flat.reshape(field.shape)


def pick(edge, index):
    safe = jnp.maximum(index, 0)
    present = (index >= 0).reshape((-1,) + (1,) * (edge.ndim - 1))
    return jnp.where(present, edge[safe], 0.0)


def reference(tracers, east_velocity, north_velocity, upward_velocity, target, bottom, shave_fraction, side_bottom, neighbors, fold_partner, thin_pairs):
    levels = jnp.arange(LEVELS, dtype=jnp.int32)
    east_flow = east_velocity[:, None]
    north_flow = north_velocity[:, None]
    west_values = pick(tracers[..., BS - 1], neighbors[:, 0])
    west_flows = pick(east_flow[..., BS - 1], neighbors[:, 0])
    east_values = pick(tracers[..., 0], neighbors[:, 1])
    east_flows = pick(east_flow[..., 0], neighbors[:, 1])
    south_values = pick(tracers[..., BS - 1, :], neighbors[:, 2])
    south_flows = pick(north_flow[..., BS - 1, :], neighbors[:, 2])
    north_values = pick(tracers[..., 0, :], neighbors[:, 3]) + pick(tracers[..., BS - 1, ::-1], fold_partner)
    north_flows = pick(north_flow[..., 0, :], neighbors[:, 3]) - pick(north_flow[..., BS - 1, ::-1], fold_partner)

    def block_totals(inputs):
        tracer_block, target_block, bottom_block, shave_block = inputs
        wet, thick = column_masks(levels, bottom_block[None], shave_block[None])
        restoring = RATE * (target_block[None] - tracer_block[None])
        return jnp.sum(jnp.where(wet, thick * restoring, 0.0)), jnp.sum(jnp.where(wet, thick, 0.0))

    sources, volumes = lax.map(block_totals, (tracers, target, bottom, shave_fraction))
    total_source = jnp.sum(sources)
    total_volume = TRACERS * jnp.sum(volumes)

    def block_step(inputs):
        (tracer_block, east_block, north_block, upward_block, target_block, bottom_block, shave_block, side_block, pairs_block,
         west_value, west_flow, east_value, east_flow_row, south_value, south_flow, north_value, north_flow_row) = inputs
        wet, thick = column_masks(levels, bottom_block[None], shave_block[None])
        tracer_one = tracer_block[None]
        advected = advected_field(tracer_one, east_block[None, None], north_block[None, None], upward_block[None, None], levels, bottom_block[None], wet, thick, side_block[None],
                                  (west_value[None], west_flow[None]), (east_value[None], east_flow_row[None]),
                                  (south_value[None], south_flow[None]), (north_value[None], north_flow_row[None]))
        restoring = RATE * (target_block[None] - tracer_one)
        stepped = jnp.where(wet, advected + restoring - total_source / total_volume, 0.0)
        return merge_block(stepped[0], bottom_block.reshape(-1), shave_block.reshape(-1), pairs_block, levels)

    return lax.map(block_step, (tracers, east_velocity, north_velocity, upward_velocity, target, bottom, shave_fraction, side_bottom, thin_pairs,
                                west_values, west_flows, east_values, east_flows, south_values, south_flows, north_values, north_flows))
```

```python
import functools

import jax
import jax.numpy as jnp
from jax import lax
from jax.experimental import pallas as pl
from jax.experimental.pallas import tpu as pltpu
from jax.sharding import PartitionSpec as P

RATE = 0.5
THIN_LIMIT = 0.35
MESH = pl.DeviceIdType.MESH
F32 = jnp.float32
HIGHEST = lax.Precision.HIGHEST


def upwind(face, first, second):
    return jnp.maximum(face, 0.0) * first + jnp.minimum(face, 0.0) * second


def kernel(
    nb,
    nl,
    nbr_ref,
    fold_ref,
    side_ref,
    t_hbm,
    u_hbm,
    v_hbm,
    w_hbm,
    g_hbm,
    bottom_hbm,
    shave_hbm,
    out_ref,
    t_ref,
    u_ref,
    v_ref,
    w_ref,
    g_ref,
    bottom_ref,
    shave_ref,
    x_ref,
    edge_ref,
    pay_ref,
    halo_ref,
    part_ref,
    parts_ref,
    in_sem,
    edge_send,
    edge_recv,
    part_send,
    part_recv,
):
    levels, rows, cols = t_ref.shape
    n = nb * nl
    block = lax.axis_index("blocks")
    lev = lax.axis_index("lev")
    me = block * nl + lev

    loads = [
        pltpu.make_async_copy(src, dst, in_sem.at[i])
        for i, (src, dst) in enumerate(
            (
                (t_hbm, t_ref),
                (u_hbm, u_ref),
                (bottom_hbm, bottom_ref),
                (shave_hbm, shave_ref),
                (g_hbm, g_ref),
                (v_hbm, v_ref),
                (w_hbm, w_ref),
            )
        )
    ]
    for load in loads:
        load.start()

    barrier = pltpu.get_barrier_semaphore()

    def greet(i, carry):
        there = lax.rem(me + i, n)
        pl.semaphore_signal(
            barrier,
            inc=1,
            device_id={"blocks": lax.div(there, nl), "lev": lax.rem(there, nl)},
            device_id_type=MESH,
        )
        return carry

    lax.fori_loop(1, n, greet, 0)

    lane = lax.broadcasted_iota(jnp.int32, (rows, cols), 1)
    row = lax.broadcasted_iota(jnp.int32, (rows, cols), 0)
    lane_pair = lane // 2

    for load in loads[:4]:
        load.wait()
    bottom = bottom_ref[...]
    shave = shave_ref[...]
    strip = jnp.zeros((rows, cols), F32)
    fields = [functools.partial(lambda k: t_ref[k], k) for k in range(levels)]
    fields += [functools.partial(lambda k: u_ref[k], k) for k in range(levels)]
    fields += [lambda: bottom.astype(F32), lambda: shave]
    for j, field in enumerate(fields):
        strip = jnp.where(lane_pair == j, pltpu.roll(field(), 2 * j + 1, 1), strip)
    edge_ref[...] = strip.T

    loads[5].wait()
    t_east = edge_ref[pl.ds(0, levels, stride=2), :]
    t_west = edge_ref[pl.ds(1, levels, stride=2), :]
    u_east = edge_ref[pl.ds(2 * levels, levels, stride=2), :]
    u_west = edge_ref[pl.ds(2 * levels + 1, levels, stride=2), :]
    t_south = t_ref[:, 0, :]
    t_north = t_ref[:, rows - 1, :]
    v_south = v_ref[:, 0, :]
    v_north = v_ref[:, rows - 1, :]
    t_edges = (t_west, t_east, t_south, t_north)
    f_edges = (u_west, u_east, v_south, v_north)
    sides = [nbr_ref[0, s] for s in range(4)]
    fold = fold_ref[0]
    blank = jnp.zeros((levels, cols), F32)

    def compose(there):
        t_side, f_side = blank, blank
        for s in range(4):
            hit = sides[s] == there
            t_side = jnp.where(hit, t_edges[s], t_side)
            f_side = jnp.where(hit, f_edges[s], f_side)
        hit = fold == there
        return t_side, f_side, jnp.where(hit, t_north, blank), jnp.where(hit, v_north, blank)

    def pack(i, carry):
        parts = compose(lax.rem(block + i, nb))
        for p, part in enumerate(parts):
            pay_ref[i - 1, p * levels : (p + 1) * levels, :] = part
        return carry

    lax.fori_loop(1, nb, pack, 0)

    loads[4].wait()
    last = bottom - 1
    source = jnp.zeros((rows, cols), F32)
    for k in range(levels):
        thick = jnp.where(k < last, 1.0, jnp.where(k == last, shave, 0.0))
        source += thick * (RATE * (g_ref[k] - t_ref[k]))
    volume = jnp.where(bottom > 0, last.astype(F32) + shave, 0.0)
    source = jnp.sum(source, axis=0, keepdims=True)
    volume = jnp.sum(volume, axis=0, keepdims=True)
    half = cols // 2
    first_half = lax.broadcasted_iota(jnp.int32, (1, cols), 1) < half
    own_part = jnp.where(
        first_half,
        source + pltpu.roll(source, half, 1),
        volume + pltpu.roll(volume, half, 1),
    )
    part_ref[...] = own_part

    pl.semaphore_wait(barrier, n - 1)

    def send_edges(i, carry):
        pltpu.make_async_remote_copy(
            src_ref=pay_ref.at[i - 1],
            dst_ref=halo_ref.at[i - 1],
            send_sem=edge_send,
            recv_sem=edge_recv,
            device_id={"blocks": lax.rem(block + i, nb), "lev": lev},
            device_id_type=MESH,
        ).start()
        return carry

    def send_part(i, carry):
        there = lax.rem(me + i, n)
        pltpu.make_async_remote_copy(
            src_ref=part_ref,
            dst_ref=parts_ref.at[i - 1],
            send_sem=part_send,
            recv_sem=part_recv,
            device_id={"blocks": lax.div(there, nl), "lev": lax.rem(there, nl)},
            device_id_type=MESH,
        ).start()
        return carry

    lax.fori_loop(1, n, send_part, 0)
    lax.fori_loop(1, nb, send_edges, 0)

    loads[6].wait()
    inverse = 1.0 / shave
    bottom_east = pltpu.roll(bottom, cols - 1, 1)
    open_east = jnp.where(lane == cols - 1, 0, jnp.minimum(bottom, bottom_east))
    open_north = jnp.where(row == rows - 1, 0, jnp.minimum(bottom, pltpu.roll(bottom, rows - 1, 0)))
    upper = jnp.zeros((rows, cols), F32)
    for k in range(levels):
        t = t_ref[k]
        u = u_ref[k]
        v = v_ref[k]
        face = jnp.where(k < open_east, 0.5 * (u + pltpu.roll(u, cols - 1, 1)), 0.0)
        flux = upwind(face, t, pltpu.roll(t, cols - 1, 1))
        divergence = pltpu.roll(flux, 1, 1) - flux
        face = jnp.where(k < open_north, 0.5 * (v + pltpu.roll(v, rows - 1, 0)), 0.0)
        flux = upwind(face, t, pltpu.roll(t, rows - 1, 0))
        divergence += pltpu.roll(flux, 1, 0) - flux
        if k < levels - 1:
            face = jnp.where(k + 1 < bottom, 0.5 * (w_ref[k] + w_ref[k + 1]), 0.0)
            lower = upwind(face, t_ref[k + 1], t)
        else:
            lower = jnp.zeros((rows, cols), F32)
        divergence += lower - upper
        upper = lower
        x_ref[k] = t + divergence * jnp.where(k == last, inverse, 1.0) + RATE * (g_ref[k] - t)

    pltpu.make_async_copy(halo_ref, halo_ref, edge_recv).wait()

    own = compose(block)
    found_t = [jnp.where(sides[s] == block, t_edges[s ^ 1], blank) for s in range(4)]
    found_f = [jnp.where(sides[s] == block, f_edges[s ^ 1], blank) for s in range(4)]

    def collect(i, carry):
        found_t, found_f, fold_t, fold_f = carry
        origin = lax.rem(block + nb - i, nb)
        side_t, side_f, over_t, over_f = (
            halo_ref[i - 1, p * levels : (p + 1) * levels, :] for p in range(4)
        )
        found_t = [jnp.where(sides[s] == origin, side_t, found_t[s]) for s in range(4)]
        found_f = [jnp.where(sides[s] == origin, side_f, found_f[s]) for s in range(4)]
        hit = fold == origin
        return found_t, found_f, jnp.where(hit, over_t, fold_t), jnp.where(hit, over_f, fold_f)

    found_t, found_f, fold_t, fold_f = lax.fori_loop(
        1, nb, collect, (found_t, found_f, own[2], own[3])
    )
    mirror = (
        lax.broadcasted_iota(jnp.int32, (cols, cols), 0)
        + lax.broadcasted_iota(jnp.int32, (cols, cols), 1)
        == cols - 1
    ).astype(F32)
    turned = jnp.dot(
        jnp.concatenate([fold_t, fold_f], 0), mirror, precision=HIGHEST, preferred_element_type=F32
    )
    found_t[3] = found_t[3] + turned[:levels]
    found_f[3] = found_f[3] - turned[levels:]

    grid = lax.broadcasted_iota(jnp.int32, (levels, cols), 0).astype(F32)
    edge_bottom = (
        edge_ref[4 * levels + 1 : 4 * levels + 2, :],
        edge_ref[4 * levels : 4 * levels + 1, :],
        bottom_ref[0:1, :].astype(F32),
        bottom_ref[rows - 1 : rows, :].astype(F32),
    )
    edge_shave = (
        edge_ref[4 * levels + 3 : 4 * levels + 4, :],
        edge_ref[4 * levels + 2 : 4 * levels + 3, :],
        shave_ref[0:1, :],
        shave_ref[rows - 1 : rows, :],
    )
    gains = []
    for s in range(4):
        beyond = side_ref[s : s + 1, :].astype(F32)
        wet = grid < jnp.minimum(edge_bottom[s], beyond)
        face = jnp.where(wet, 0.5 * (f_edges[s] + found_f[s]), 0.0)
        if s % 2 == 0:
            flux = upwind(face, found_t[s], t_edges[s])
        else:
            flux = -upwind(face, t_edges[s], found_t[s])
        gains.append(flux * jnp.where(grid == edge_bottom[s] - 1.0, 1.0 / edge_shave[s], 1.0))
    for k in range(levels):
        x_ref[k, 0:1, :] += gains[2][k : k + 1, :]
        x_ref[k, rows - 1 : rows, :] += gains[3][k : k + 1, :]
    wide = jnp.concatenate(gains[:2], 0)
    place = lax.broadcasted_iota(jnp.int32, (2 * levels, cols), 0)
    place_lane = lax.broadcasted_iota(jnp.int32, (2 * levels, cols), 1)

    partner_shave = jnp.where(bottom_east == bottom, pltpu.roll(shave, cols - 1, 1), 1.0)
    scale = 1.0 / (shave + partner_shave)
    weight = shave * scale
    partner_weight = partner_shave * scale
    struck = jnp.where(shave < THIN_LIMIT, last, -1)
    struck_west = pltpu.roll(struck, 1, 1)

    pltpu.make_async_copy(parts_ref, parts_ref, part_recv).wait()
    total = lax.fori_loop(0, n - 1, lambda i, carry: carry + parts_ref[i], own_part)
    total_source = jnp.sum(jnp.where(first_half, total, 0.0), axis=1, keepdims=True)
    total_volume = jnp.sum(jnp.where(first_half, 0.0, total), axis=1, keepdims=True)
    mean = total_source / total_volume

    for k in range(levels):
        chosen = (place == k) & (place_lane == 0) | (place == levels + k) & (place_lane == cols - 1)
        side_gain = lax.dot_general(
            wide,
            chosen.astype(F32),
            (((0,), (0,)), ((), ())),
            precision=HIGHEST,
            preferred_element_type=F32,
        )
        x = x_ref[k] + side_gain
        merged = weight * x + partner_weight * pltpu.roll(x, cols - 1, 1)
        x = jnp.where(struck == k, merged, x)
        x = jnp.where(struck_west == k, pltpu.roll(merged, 1, 1), x)
        out_ref[k] = jnp.where(k < bottom, x - mean, 0.0)

    pltpu.make_async_copy(halo_ref, halo_ref, edge_send).wait()
    pltpu.make_async_copy(parts_ref, parts_ref, part_send).wait()


def local(
    nb,
    nl,
    tracers,
    east_velocity,
    north_velocity,
    upward_velocity,
    target,
    bottom,
    shave_fraction,
    side_bottom,
    neighbors,
    fold_partner,
    thin_pairs,
):
    levels, rows, cols = tracers.shape[2:]
    cube = (levels, rows, cols)
    n = nb * nl
    smem = pl.BlockSpec(memory_space=pltpu.SMEM)
    vmem = pl.BlockSpec(memory_space=pltpu.VMEM)
    anywhere = pl.BlockSpec(memory_space=pl.ANY)
    stepped = pl.pallas_call(
        functools.partial(kernel, nb, nl),
        out_shape=jax.ShapeDtypeStruct(cube, F32),
        in_specs=[smem, smem, vmem] + [anywhere] * 7,
        out_specs=vmem,
        scratch_shapes=[
            pltpu.VMEM(cube, F32),
            pltpu.VMEM(cube, F32),
            pltpu.VMEM(cube, F32),
            pltpu.VMEM(cube, F32),
            pltpu.VMEM(cube, F32),
            pltpu.VMEM((rows, cols), jnp.int32),
            pltpu.VMEM((rows, cols), F32),
            pltpu.VMEM(cube, F32),
            pltpu.VMEM((cols, rows), F32),
            pltpu.VMEM((nb - 1, 4 * levels, cols), F32),
            pltpu.VMEM((nb - 1, 4 * levels, cols), F32),
            pltpu.VMEM((1, cols), F32),
            pltpu.VMEM((n - 1, 1, cols), F32),
            pltpu.SemaphoreType.DMA((7,)),
            pltpu.SemaphoreType.DMA,
            pltpu.SemaphoreType.DMA,
            pltpu.SemaphoreType.DMA,
            pltpu.SemaphoreType.DMA,
        ],
        compiler_params=pltpu.CompilerParams(collective_id=0, has_side_effects=True),
    )(
        neighbors,
        fold_partner,
        side_bottom.reshape(4, cols),
        tracers.reshape(cube),
        east_velocity.reshape(cube),
        north_velocity.reshape(cube),
        upward_velocity.reshape(cube),
        target.reshape(cube),
        bottom.reshape(rows, cols),
        shave_fraction.reshape(rows, cols),
    )
    return stepped.reshape(tracers.shape)


def solution(mesh):
    placed = (
        P("blocks", "lev", None, None, None),
        P("blocks", None, None, None),
        P("blocks", None, None, None),
        P("blocks", None, None, None),
        P("blocks", "lev", None, None, None),
        P("blocks", None, None),
        P("blocks", None, None),
        P("blocks", None, None),
        P("blocks", None),
        P("blocks"),
        P("blocks", None, None),
    )
    return jax.shard_map(
        functools.partial(local, mesh.shape["blocks"], mesh.shape["lev"]),
        mesh=mesh,
        in_specs=placed,
        out_specs=P("blocks", "lev", None, None, None),
        check_vma=False,
    )
```

```python
import functools

import jax
import jax.numpy as jnp
from jax import lax
from jax.experimental import pallas as pl
from jax.experimental.pallas import tpu as pltpu
from jax.sharding import PartitionSpec as P

RATE = 0.5
THIN_LIMIT = 0.35
MESH = pl.DeviceIdType.MESH
F32 = jnp.float32
HIGHEST = lax.Precision.HIGHEST


def upwind(face, first, second):
    return jnp.maximum(face, 0.0) * first + jnp.minimum(face, 0.0) * second


def kernel(
    nb,
    nl,
    nbr_hbm,
    fold_hbm,
    side_hbm,
    t_hbm,
    u_hbm,
    v_hbm,
    w_hbm,
    g_hbm,
    bottom_hbm,
    shave_hbm,
    out_ref,
    t_ref,
    u_ref,
    v_ref,
    w_ref,
    g_ref,
    bottom_ref,
    shave_ref,
    nbr_ref,
    fold_ref,
    side_ref,
    x_ref,
    edge_ref,
    pay_ref,
    halo_ref,
    part_ref,
    parts_ref,
    in_sem,
    edge_send,
    edge_recv,
    part_send,
    part_recv,
):
    levels, rows, cols = t_ref.shape
    n = nb * nl
    unroll = n <= 64
    block = lax.axis_index("blocks")
    lev = lax.axis_index("lev")

    def each_other(visit):
        def outer(i, carry):
            there = lax.rem(block + i, nb)

            def inner(j, carry):
                visit(i * nl + j - 1, {"blocks": there, "lev": lax.rem(lev + j, nl)})
                return carry

            return lax.fori_loop(0, nl, inner, carry, unroll=unroll)

        def first(j, carry):
            visit(j - 1, {"blocks": block, "lev": lax.rem(lev + j, nl)})
            return carry

        lax.fori_loop(1, nb, outer, 0, unroll=unroll)
        lax.fori_loop(1, nl, first, 0, unroll=unroll)

    loads = [
        pltpu.make_async_copy(src, dst, in_sem.at[i])
        for i, (src, dst) in enumerate(
            (
                (t_hbm, t_ref),
                (u_hbm, u_ref),
                (bottom_hbm, bottom_ref),
                (shave_hbm, shave_ref),
                (g_hbm, g_ref),
                (v_hbm, v_ref),
                (w_hbm, w_ref),
                (nbr_hbm, nbr_ref),
                (fold_hbm, fold_ref),
                (side_hbm, side_ref),
            )
        )
    ]
    for load in loads:
        load.start()

    barrier = pltpu.get_barrier_semaphore()

    each_other(
        lambda slot, device: pl.semaphore_signal(
            barrier, inc=1, device_id=device, device_id_type=MESH
        )
    )

    lane = lax.broadcasted_iota(jnp.int32, (rows, cols), 1)
    row = lax.broadcasted_iota(jnp.int32, (rows, cols), 0)
    lane_pair = lane // 2

    for load in loads[:4]:
        load.wait()
    bottom = bottom_ref[...]
    shave = shave_ref[...]
    strip = jnp.zeros((rows, cols), F32)
    fields = [functools.partial(lambda k: t_ref[k], k) for k in range(levels)]
    fields += [functools.partial(lambda k: u_ref[k], k) for k in range(levels)]
    fields += [lambda: bottom.astype(F32), lambda: shave]
    for j, field in enumerate(fields):
        strip = jnp.where(lane_pair == j, pltpu.roll(field(), 2 * j + 1, 1), strip)
    edge_ref[...] = strip.T

    loads[5].wait()
    loads[7].wait()
    loads[8].wait()
    loads[9].wait()
    t_east = edge_ref[pl.ds(0, levels, stride=2), :]
    t_west = edge_ref[pl.ds(1, levels, stride=2), :]
    u_east = edge_ref[pl.ds(2 * levels, levels, stride=2), :]
    u_west = edge_ref[pl.ds(2 * levels + 1, levels, stride=2), :]
    t_south = t_ref[:, 0, :]
    t_north = t_ref[:, rows - 1, :]
    v_south = v_ref[:, 0, :]
    v_north = v_ref[:, rows - 1, :]
    t_edges = (t_west, t_east, t_south, t_north)
    f_edges = (u_west, u_east, v_south, v_north)
    sides = [nbr_ref[0, s] for s in range(4)]
    fold = fold_ref[0, 0]
    blank = jnp.zeros((levels, cols), F32)

    def compose(there):
        t_side, f_side = blank, blank
        for s in range(4):
            hit = sides[s] == there
            t_side = jnp.where(hit, t_edges[s], t_side)
            f_side = jnp.where(hit, f_edges[s], f_side)
        hit = fold == there
        return t_side, f_side, jnp.where(hit, t_north, blank), jnp.where(hit, v_north, blank)

    def pack(i, carry):
        parts = compose(lax.rem(block + i, nb))
        for p, part in enumerate(parts):
            pay_ref[i - 1, p * levels : (p + 1) * levels, :] = part
        return carry

    lax.fori_loop(1, nb, pack, 0, unroll=unroll)

    loads[4].wait()
    last = bottom - 1
    source = jnp.zeros((rows, cols), F32)
    for k in range(levels):
        thick = jnp.where(k < last, 1.0, jnp.where(k == last, shave, 0.0))
        source += thick * (RATE * (g_ref[k] - t_ref[k]))
    volume = jnp.where(bottom > 0, last.astype(F32) + shave, 0.0)
    source = jnp.sum(source, axis=0, keepdims=True)
    volume = jnp.sum(volume, axis=0, keepdims=True)
    half = cols // 2
    first_half = lax.broadcasted_iota(jnp.int32, (1, cols), 1) < half
    own_part = jnp.where(
        first_half,
        source + pltpu.roll(source, half, 1),
        volume + pltpu.roll(volume, half, 1),
    )
    part_ref[...] = own_part

    pl.semaphore_wait(barrier, n - 1)

    def send_edges(i, carry):
        pltpu.make_async_remote_copy(
            src_ref=pay_ref.at[i - 1],
            dst_ref=halo_ref.at[i - 1],
            send_sem=edge_send,
            recv_sem=edge_recv,
            device_id={"blocks": lax.rem(block + i, nb), "lev": lev},
            device_id_type=MESH,
        ).start()
        return carry

    each_other(
        lambda slot, device: pltpu.make_async_remote_copy(
            src_ref=part_ref,
            dst_ref=parts_ref.at[slot],
            send_sem=part_send,
            recv_sem=part_recv,
            device_id=device,
            device_id_type=MESH,
        ).start()
    )
    lax.fori_loop(1, nb, send_edges, 0, unroll=unroll)

    loads[6].wait()
    inverse = 1.0 / shave
    bottom_east = pltpu.roll(bottom, cols - 1, 1)
    open_east = jnp.where(lane == cols - 1, 0, jnp.minimum(bottom, bottom_east))
    open_north = jnp.where(row == rows - 1, 0, jnp.minimum(bottom, pltpu.roll(bottom, rows - 1, 0)))
    upper = jnp.zeros((rows, cols), F32)
    for k in range(levels):
        t = t_ref[k]
        u = u_ref[k]
        v = v_ref[k]
        face = jnp.where(k < open_east, 0.5 * (u + pltpu.roll(u, cols - 1, 1)), 0.0)
        flux = upwind(face, t, pltpu.roll(t, cols - 1, 1))
        divergence = pltpu.roll(flux, 1, 1) - flux
        face = jnp.where(k < open_north, 0.5 * (v + pltpu.roll(v, rows - 1, 0)), 0.0)
        flux = upwind(face, t, pltpu.roll(t, rows - 1, 0))
        divergence += pltpu.roll(flux, 1, 0) - flux
        if k < levels - 1:
            face = jnp.where(k + 1 < bottom, 0.5 * (w_ref[k] + w_ref[k + 1]), 0.0)
            lower = upwind(face, t_ref[k + 1], t)
        else:
            lower = jnp.zeros((rows, cols), F32)
        divergence += lower - upper
        upper = lower
        x_ref[k] = t + divergence * jnp.where(k == last, inverse, 1.0) + RATE * (g_ref[k] - t)

    pltpu.make_async_copy(halo_ref, halo_ref, edge_recv).wait()

    own = compose(block)
    found_t = [jnp.where(sides[s] == block, t_edges[s ^ 1], blank) for s in range(4)]
    found_f = [jnp.where(sides[s] == block, f_edges[s ^ 1], blank) for s in range(4)]

    def collect(i, carry):
        found_t, found_f, fold_t, fold_f = carry
        origin = lax.rem(block + nb - i, nb)
        side_t, side_f, over_t, over_f = (
            halo_ref[i - 1, p * levels : (p + 1) * levels, :] for p in range(4)
        )
        found_t = [jnp.where(sides[s] == origin, side_t, found_t[s]) for s in range(4)]
        found_f = [jnp.where(sides[s] == origin, side_f, found_f[s]) for s in range(4)]
        hit = fold == origin
        return found_t, found_f, jnp.where(hit, over_t, fold_t), jnp.where(hit, over_f, fold_f)

    found_t, found_f, fold_t, fold_f = lax.fori_loop(
        1, nb, collect, (found_t, found_f, own[2], own[3]), unroll=unroll
    )
    mirror = (
        lax.broadcasted_iota(jnp.int32, (cols, cols), 0)
        + lax.broadcasted_iota(jnp.int32, (cols, cols), 1)
        == cols - 1
    ).astype(F32)
    turned = jnp.dot(
        jnp.concatenate([fold_t, fold_f], 0), mirror, precision=HIGHEST, preferred_element_type=F32
    )
    found_t[3] = found_t[3] + turned[:levels]
    found_f[3] = found_f[3] - turned[levels:]

    grid = lax.broadcasted_iota(jnp.int32, (levels, cols), 0).astype(F32)
    edge_bottom = (
        edge_ref[4 * levels + 1 : 4 * levels + 2, :],
        edge_ref[4 * levels : 4 * levels + 1, :],
        bottom_ref[0:1, :].astype(F32),
        bottom_ref[rows - 1 : rows, :].astype(F32),
    )
    edge_shave = (
        edge_ref[4 * levels + 3 : 4 * levels + 4, :],
        edge_ref[4 * levels + 2 : 4 * levels + 3, :],
        shave_ref[0:1, :],
        shave_ref[rows - 1 : rows, :],
    )
    gains = []
    for s in range(4):
        beyond = side_ref[s : s + 1, :].astype(F32)
        wet = grid < jnp.minimum(edge_bottom[s], beyond)
        face = jnp.where(wet, 0.5 * (f_edges[s] + found_f[s]), 0.0)
        if s % 2 == 0:
            flux = upwind(face, found_t[s], t_edges[s])
        else:
            flux = -upwind(face, t_edges[s], found_t[s])
        gains.append(flux * jnp.where(grid == edge_bottom[s] - 1.0, 1.0 / edge_shave[s], 1.0))
    for k in range(levels):
        x_ref[k, 0:1, :] += gains[2][k : k + 1, :]
        x_ref[k, rows - 1 : rows, :] += gains[3][k : k + 1, :]
    wide = jnp.concatenate(gains[:2], 0)
    place = lax.broadcasted_iota(jnp.int32, (2 * levels, cols), 0)
    place_lane = lax.broadcasted_iota(jnp.int32, (2 * levels, cols), 1)

    partner_shave = jnp.where(bottom_east == bottom, pltpu.roll(shave, cols - 1, 1), 1.0)
    scale = 1.0 / (shave + partner_shave)
    weight = shave * scale
    partner_weight = partner_shave * scale
    struck = jnp.where(shave < THIN_LIMIT, last, -1)
    struck_west = pltpu.roll(struck, 1, 1)

    for k in range(levels):
        chosen = (place == k) & (place_lane == 0) | (place == levels + k) & (place_lane == cols - 1)
        side_gain = lax.dot_general(
            wide,
            chosen.astype(F32),
            (((0,), (0,)), ((), ())),
            precision=HIGHEST,
            preferred_element_type=F32,
        )
        x = x_ref[k] + side_gain
        merged = weight * x + partner_weight * pltpu.roll(x, cols - 1, 1)
        x = jnp.where(struck == k, merged, x)
        x = jnp.where(struck_west == k, pltpu.roll(merged, 1, 1), x)
        x_ref[k] = x

    pltpu.make_async_copy(parts_ref, parts_ref, part_recv).wait()
    total = lax.fori_loop(
        0, n - 1, lambda i, carry: carry + parts_ref[i], own_part, unroll=unroll
    )
    total_source = jnp.sum(jnp.where(first_half, total, 0.0), axis=1, keepdims=True)
    total_volume = jnp.sum(jnp.where(first_half, 0.0, total), axis=1, keepdims=True)
    mean = total_source / total_volume

    for k in range(levels):
        out_ref[k] = jnp.where(k < bottom, x_ref[k] - mean, 0.0)

    pltpu.make_async_copy(halo_ref, halo_ref, edge_send).wait()
    pltpu.make_async_copy(parts_ref, parts_ref, part_send).wait()


def local(
    nb,
    nl,
    tracers,
    east_velocity,
    north_velocity,
    upward_velocity,
    target,
    bottom,
    shave_fraction,
    side_bottom,
    neighbors,
    fold_partner,
    thin_pairs,
):
    levels, rows, cols = tracers.shape[2:]
    in_hbm = functools.partial(pltpu.with_memory_space_constraint, memory_space=pltpu.HBM)
    cube = (levels, rows, cols)
    n = nb * nl
    vmem = pl.BlockSpec(memory_space=pltpu.VMEM)
    grant = (12 << 20) + 4 * cols * (8 * levels * nb + 8 * n)
    anywhere = pl.BlockSpec(memory_space=pl.ANY)
    stepped = pl.pallas_call(
        functools.partial(kernel, nb, nl),
        out_shape=pltpu.VMEM(cube, F32),
        in_specs=[anywhere] * 10,
        out_specs=vmem,
        scratch_shapes=[
            pltpu.VMEM(cube, F32),
            pltpu.VMEM(cube, F32),
            pltpu.VMEM(cube, F32),
            pltpu.VMEM(cube, F32),
            pltpu.VMEM(cube, F32),
            pltpu.VMEM((rows, cols), jnp.int32),
            pltpu.VMEM((rows, cols), F32),
            pltpu.SMEM((1, 4), jnp.int32),
            pltpu.SMEM((1, 1), jnp.int32),
            pltpu.VMEM((4, cols), jnp.int32),
            pltpu.VMEM(cube, F32),
            pltpu.VMEM((cols, rows), F32),
            pltpu.VMEM((nb - 1, 4 * levels, cols), F32),
            pltpu.VMEM((nb - 1, 4 * levels, cols), F32),
            pltpu.VMEM((1, cols), F32),
            pltpu.VMEM((n - 1, 1, cols), F32),
            pltpu.SemaphoreType.DMA((10,)),
            pltpu.SemaphoreType.DMA,
            pltpu.SemaphoreType.DMA,
            pltpu.SemaphoreType.DMA,
            pltpu.SemaphoreType.DMA,
        ],
        compiler_params=pltpu.CompilerParams(
            collective_id=0, has_side_effects=True, vmem_limit_bytes=grant
        ),
    )(
        in_hbm(neighbors),
        fold_partner.reshape(1, 1),
        in_hbm(side_bottom.reshape(4, cols)),
        in_hbm(tracers.reshape(cube)),
        in_hbm(east_velocity.reshape(cube)),
        in_hbm(north_velocity.reshape(cube)),
        in_hbm(upward_velocity.reshape(cube)),
        in_hbm(target.reshape(cube)),
        in_hbm(bottom.reshape(rows, cols)),
        in_hbm(shave_fraction.reshape(rows, cols)),
    )
    return stepped.reshape(tracers.shape)


def solution(mesh):
    placed = (
        P("blocks", "lev", None, None, None),
        P("blocks", None, None, None),
        P("blocks", None, None, None),
        P("blocks", None, None, None),
        P("blocks", "lev", None, None, None),
        P("blocks", None, None),
        P("blocks", None, None),
        P("blocks", None, None),
        P("blocks", None),
        P("blocks"),
        P("blocks", None, None),
    )
    return jax.shard_map(
        functools.partial(local, mesh.shape["blocks"], mesh.shape["lev"]),
        mesh=mesh,
        in_specs=placed,
        out_specs=P("blocks", "lev", None, None, None),
        check_vma=False,
    )
```

```python
import functools

import jax
import jax.numpy as jnp
from jax import lax
from jax.experimental import pallas as pl
from jax.experimental.pallas import tpu as pltpu
from jax.sharding import PartitionSpec as P

RATE = 0.5
THIN_LIMIT = 0.35
MESH = pl.DeviceIdType.MESH
F32 = jnp.float32
HIGHEST = lax.Precision.HIGHEST


def upwind(face, first, second):
    return jnp.maximum(face, 0.0) * first + jnp.minimum(face, 0.0) * second


def kernel(
    nb,
    nl,
    nbr_hbm,
    fold_hbm,
    side_hbm,
    t_hbm,
    u_hbm,
    v_hbm,
    w_hbm,
    g_hbm,
    bottom_hbm,
    shave_hbm,
    out_ref,
    t_ref,
    u_ref,
    v_ref,
    w_ref,
    g_ref,
    bottom_ref,
    shave_ref,
    nbr_ref,
    fold_ref,
    side_ref,
    x_ref,
    edge_ref,
    pay_ref,
    halo_ref,
    group_ref,
    parts_ref,
    in_sem,
    edge_send,
    edge_recv,
    group_send,
    group_recv,
    part_send,
    part_recv,
):
    levels, rows, cols = t_ref.shape
    n = nb * nl
    unroll = n <= 64
    block = lax.axis_index("blocks")
    lev = lax.axis_index("lev")

    def block_peers(visit):
        def step(i, carry):
            visit(i - 1, {"blocks": lax.rem(block + i, nb), "lev": lev})
            return carry

        lax.fori_loop(1, nb, step, 0, unroll=unroll)

    def lev_peers(visit):
        def step(i, carry):
            visit(i - 1, {"blocks": block, "lev": lax.rem(lev + i, nl)})
            return carry

        lax.fori_loop(1, nl, step, 0, unroll=unroll)

    loads = [
        pltpu.make_async_copy(src, dst, in_sem.at[i])
        for i, (src, dst) in enumerate(
            (
                (t_hbm, t_ref),
                (u_hbm, u_ref),
                (bottom_hbm, bottom_ref),
                (shave_hbm, shave_ref),
                (g_hbm, g_ref),
                (v_hbm, v_ref),
                (w_hbm, w_ref),
                (nbr_hbm, nbr_ref),
                (fold_hbm, fold_ref),
                (side_hbm, side_ref),
            )
        )
    ]
    for load in loads:
        load.start()

    barrier = pltpu.get_barrier_semaphore()

    def greet(slot, device):
        pl.semaphore_signal(barrier, inc=1, device_id=device, device_id_type=MESH)

    block_peers(greet)
    lev_peers(greet)

    lane = lax.broadcasted_iota(jnp.int32, (rows, cols), 1)
    row = lax.broadcasted_iota(jnp.int32, (rows, cols), 0)
    lane_pair = lane // 2

    for load in loads[:4]:
        load.wait()
    bottom = bottom_ref[...]
    shave = shave_ref[...]
    strip = jnp.zeros((rows, cols), F32)
    fields = [functools.partial(lambda k: t_ref[k], k) for k in range(levels)]
    fields += [functools.partial(lambda k: u_ref[k], k) for k in range(levels)]
    fields += [lambda: bottom.astype(F32), lambda: shave]
    for j, field in enumerate(fields):
        strip = jnp.where(lane_pair == j, pltpu.roll(field(), 2 * j + 1, 1), strip)
    edge_ref[...] = strip.T

    loads[5].wait()
    loads[7].wait()
    loads[8].wait()
    loads[9].wait()
    t_east = edge_ref[pl.ds(0, levels, stride=2), :]
    t_west = edge_ref[pl.ds(1, levels, stride=2), :]
    u_east = edge_ref[pl.ds(2 * levels, levels, stride=2), :]
    u_west = edge_ref[pl.ds(2 * levels + 1, levels, stride=2), :]
    t_south = t_ref[:, 0, :]
    t_north = t_ref[:, rows - 1, :]
    v_south = v_ref[:, 0, :]
    v_north = v_ref[:, rows - 1, :]
    t_edges = (t_west, t_east, t_south, t_north)
    f_edges = (u_west, u_east, v_south, v_north)
    sides = [nbr_ref[0, s] for s in range(4)]
    fold = fold_ref[0, 0]
    blank = jnp.zeros((levels, cols), F32)

    def compose(there):
        t_side, f_side = blank, blank
        for s in range(4):
            hit = sides[s] == there
            t_side = jnp.where(hit, t_edges[s], t_side)
            f_side = jnp.where(hit, f_edges[s], f_side)
        hit = fold == there
        return t_side, f_side, jnp.where(hit, t_north, blank), jnp.where(hit, v_north, blank)

    def pack(i, carry):
        parts = compose(lax.rem(block + i, nb))
        for p, part in enumerate(parts):
            pay_ref[i - 1, p * levels : (p + 1) * levels, :] = part
        return carry

    lax.fori_loop(1, nb, pack, 0, unroll=unroll)

    loads[4].wait()
    last = bottom - 1
    source = jnp.zeros((rows, cols), F32)
    for k in range(levels):
        thick = jnp.where(k < last, 1.0, jnp.where(k == last, shave, 0.0))
        source += thick * (RATE * (g_ref[k] - t_ref[k]))
    volume = jnp.where(bottom > 0, last.astype(F32) + shave, 0.0)
    source = jnp.sum(source, axis=0, keepdims=True)
    volume = jnp.sum(volume, axis=0, keepdims=True)
    half = cols // 2
    first_half = lax.broadcasted_iota(jnp.int32, (1, cols), 1) < half
    own_part = jnp.where(
        first_half,
        source + pltpu.roll(source, half, 1),
        volume + pltpu.roll(volume, half, 1),
    )
    group_ref[nl - 1] = own_part

    pl.semaphore_wait(barrier, nb + nl - 2)

    def send(src, dst, sems, device):
        pltpu.make_async_remote_copy(
            src_ref=src,
            dst_ref=dst,
            send_sem=sems[0],
            recv_sem=sems[1],
            device_id=device,
            device_id_type=MESH,
        ).start()

    lev_peers(
        lambda slot, device: send(
            group_ref.at[nl - 1], group_ref.at[slot], (group_send, group_recv), device
        )
    )
    block_peers(
        lambda slot, device: send(
            pay_ref.at[slot], halo_ref.at[slot], (edge_send, edge_recv), device
        )
    )

    loads[6].wait()
    inverse = 1.0 / shave
    bottom_east = pltpu.roll(bottom, cols - 1, 1)
    open_east = jnp.where(lane == cols - 1, 0, jnp.minimum(bottom, bottom_east))
    open_north = jnp.where(row == rows - 1, 0, jnp.minimum(bottom, pltpu.roll(bottom, rows - 1, 0)))
    upper = jnp.zeros((rows, cols), F32)
    received = group_ref.at[0 : nl - 1]
    for k in range(levels):
        if k == levels // 2:
            pltpu.make_async_copy(received, received, group_recv).wait()
            block_peers(
                lambda slot, device: send(
                    group_ref, parts_ref.at[slot], (part_send, part_recv), device
                )
            )
        t = t_ref[k]
        u = u_ref[k]
        v = v_ref[k]
        face = jnp.where(k < open_east, 0.5 * (u + pltpu.roll(u, cols - 1, 1)), 0.0)
        flux = upwind(face, t, pltpu.roll(t, cols - 1, 1))
        divergence = pltpu.roll(flux, 1, 1) - flux
        face = jnp.where(k < open_north, 0.5 * (v + pltpu.roll(v, rows - 1, 0)), 0.0)
        flux = upwind(face, t, pltpu.roll(t, rows - 1, 0))
        divergence += pltpu.roll(flux, 1, 0) - flux
        if k < levels - 1:
            face = jnp.where(k + 1 < bottom, 0.5 * (w_ref[k] + w_ref[k + 1]), 0.0)
            lower = upwind(face, t_ref[k + 1], t)
        else:
            lower = jnp.zeros((rows, cols), F32)
        divergence += lower - upper
        upper = lower
        x_ref[k] = t + divergence * jnp.where(k == last, inverse, 1.0) + RATE * (g_ref[k] - t)

    pltpu.make_async_copy(halo_ref, halo_ref, edge_recv).wait()

    own = compose(block)
    found_t = [jnp.where(sides[s] == block, t_edges[s ^ 1], blank) for s in range(4)]
    found_f = [jnp.where(sides[s] == block, f_edges[s ^ 1], blank) for s in range(4)]

    def collect(i, carry):
        found_t, found_f, fold_t, fold_f = carry
        origin = lax.rem(block + nb - i, nb)
        side_t, side_f, over_t, over_f = (
            halo_ref[i - 1, p * levels : (p + 1) * levels, :] for p in range(4)
        )
        found_t = [jnp.where(sides[s] == origin, side_t, found_t[s]) for s in range(4)]
        found_f = [jnp.where(sides[s] == origin, side_f, found_f[s]) for s in range(4)]
        hit = fold == origin
        return found_t, found_f, jnp.where(hit, over_t, fold_t), jnp.where(hit, over_f, fold_f)

    found_t, found_f, fold_t, fold_f = lax.fori_loop(
        1, nb, collect, (found_t, found_f, own[2], own[3]), unroll=unroll
    )
    mirror = (
        lax.broadcasted_iota(jnp.int32, (cols, cols), 0)
        + lax.broadcasted_iota(jnp.int32, (cols, cols), 1)
        == cols - 1
    ).astype(F32)
    turned = jnp.dot(
        jnp.concatenate([fold_t, fold_f], 0), mirror, precision=HIGHEST, preferred_element_type=F32
    )
    found_t[3] = found_t[3] + turned[:levels]
    found_f[3] = found_f[3] - turned[levels:]

    grid = lax.broadcasted_iota(jnp.int32, (levels, cols), 0).astype(F32)
    edge_bottom = (
        edge_ref[4 * levels + 1 : 4 * levels + 2, :],
        edge_ref[4 * levels : 4 * levels + 1, :],
        bottom_ref[0:1, :].astype(F32),
        bottom_ref[rows - 1 : rows, :].astype(F32),
    )
    edge_shave = (
        edge_ref[4 * levels + 3 : 4 * levels + 4, :],
        edge_ref[4 * levels + 2 : 4 * levels + 3, :],
        shave_ref[0:1, :],
        shave_ref[rows - 1 : rows, :],
    )
    gains = []
    for s in range(4):
        beyond = side_ref[s : s + 1, :].astype(F32)
        wet = grid < jnp.minimum(edge_bottom[s], beyond)
        face = jnp.where(wet, 0.5 * (f_edges[s] + found_f[s]), 0.0)
        if s % 2 == 0:
            flux = upwind(face, found_t[s], t_edges[s])
        else:
            flux = -upwind(face, t_edges[s], found_t[s])
        gains.append(flux * jnp.where(grid == edge_bottom[s] - 1.0, 1.0 / edge_shave[s], 1.0))
    for k in range(levels):
        x_ref[k, 0:1, :] += gains[2][k : k + 1, :]
        x_ref[k, rows - 1 : rows, :] += gains[3][k : k + 1, :]
    wide = jnp.concatenate(gains[:2], 0)
    place = lax.broadcasted_iota(jnp.int32, (2 * levels, cols), 0)
    place_lane = lax.broadcasted_iota(jnp.int32, (2 * levels, cols), 1)

    partner_shave = jnp.where(bottom_east == bottom, pltpu.roll(shave, cols - 1, 1), 1.0)
    scale = 1.0 / (shave + partner_shave)
    weight = shave * scale
    partner_weight = partner_shave * scale
    struck = jnp.where(shave < THIN_LIMIT, last, -1)
    struck_west = pltpu.roll(struck, 1, 1)

    for k in range(levels):
        chosen = (place == k) & (place_lane == 0) | (place == levels + k) & (place_lane == cols - 1)
        side_gain = lax.dot_general(
            wide,
            chosen.astype(F32),
            (((0,), (0,)), ((), ())),
            precision=HIGHEST,
            preferred_element_type=F32,
        )
        x = x_ref[k] + side_gain
        merged = weight * x + partner_weight * pltpu.roll(x, cols - 1, 1)
        x = jnp.where(struck == k, merged, x)
        x = jnp.where(struck_west == k, pltpu.roll(merged, 1, 1), x)
        x_ref[k] = x

    pltpu.make_async_copy(parts_ref, parts_ref, part_recv).wait()
    total = jnp.sum(group_ref[...], axis=0)
    total = lax.fori_loop(
        0, nb - 1, lambda i, carry: carry + jnp.sum(parts_ref[i], axis=0), total, unroll=unroll
    )
    total_source = jnp.sum(jnp.where(first_half, total, 0.0), axis=1, keepdims=True)
    total_volume = jnp.sum(jnp.where(first_half, 0.0, total), axis=1, keepdims=True)
    mean = total_source / total_volume

    for k in range(levels):
        out_ref[k] = jnp.where(k < bottom, x_ref[k] - mean, 0.0)

    pltpu.make_async_copy(halo_ref, halo_ref, edge_send).wait()
    pltpu.make_async_copy(received, received, group_send).wait()
    pltpu.make_async_copy(parts_ref, parts_ref, part_send).wait()


def local(
    nb,
    nl,
    tracers,
    east_velocity,
    north_velocity,
    upward_velocity,
    target,
    bottom,
    shave_fraction,
    side_bottom,
    neighbors,
    fold_partner,
    thin_pairs,
):
    levels, rows, cols = tracers.shape[2:]
    in_hbm = functools.partial(pltpu.with_memory_space_constraint, memory_space=pltpu.HBM)
    cube = (levels, rows, cols)
    n = nb * nl
    vmem = pl.BlockSpec(memory_space=pltpu.VMEM)
    grant = (12 << 20) + 4 * cols * (8 * levels * nb + 8 * n)
    anywhere = pl.BlockSpec(memory_space=pl.ANY)
    stepped = pl.pallas_call(
        functools.partial(kernel, nb, nl),
        out_shape=pltpu.VMEM(cube, F32),
        in_specs=[anywhere] * 10,
        out_specs=vmem,
        scratch_shapes=[
            pltpu.VMEM(cube, F32),
            pltpu.VMEM(cube, F32),
            pltpu.VMEM(cube, F32),
            pltpu.VMEM(cube, F32),
            pltpu.VMEM(cube, F32),
            pltpu.VMEM((rows, cols), jnp.int32),
            pltpu.VMEM((rows, cols), F32),
            pltpu.SMEM((1, 4), jnp.int32),
            pltpu.SMEM((1, 1), jnp.int32),
            pltpu.VMEM((4, cols), jnp.int32),
            pltpu.VMEM(cube, F32),
            pltpu.VMEM((cols, rows), F32),
            pltpu.VMEM((nb - 1, 4 * levels, cols), F32),
            pltpu.VMEM((nb - 1, 4 * levels, cols), F32),
            pltpu.VMEM((nl, 1, cols), F32),
            pltpu.VMEM((nb - 1, nl, 1, cols), F32),
            pltpu.SemaphoreType.DMA((10,)),
            pltpu.SemaphoreType.DMA,
            pltpu.SemaphoreType.DMA,
            pltpu.SemaphoreType.DMA,
            pltpu.SemaphoreType.DMA,
            pltpu.SemaphoreType.DMA,
            pltpu.SemaphoreType.DMA,
        ],
        compiler_params=pltpu.CompilerParams(
            collective_id=0, has_side_effects=True, vmem_limit_bytes=grant
        ),
    )(
        in_hbm(neighbors),
        fold_partner.reshape(1, 1),
        in_hbm(side_bottom.reshape(4, cols)),
        in_hbm(tracers.reshape(cube)),
        in_hbm(east_velocity.reshape(cube)),
        in_hbm(north_velocity.reshape(cube)),
        in_hbm(upward_velocity.reshape(cube)),
        in_hbm(target.reshape(cube)),
        in_hbm(bottom.reshape(rows, cols)),
        in_hbm(shave_fraction.reshape(rows, cols)),
    )
    return stepped.reshape(tracers.shape)


def solution(mesh):
    placed = (
        P("blocks", "lev", None, None, None),
        P("blocks", None, None, None),
        P("blocks", None, None, None),
        P("blocks", None, None, None),
        P("blocks", "lev", None, None, None),
        P("blocks", None, None),
        P("blocks", None, None),
        P("blocks", None, None),
        P("blocks", None),
        P("blocks"),
        P("blocks", None, None),
    )
    return jax.shard_map(
        functools.partial(local, mesh.shape["blocks"], mesh.shape["lev"]),
        mesh=mesh,
        in_specs=placed,
        out_specs=P("blocks", "lev", None, None, None),
        check_vma=False,
    )
```

```python
import functools

import jax
import jax.numpy as jnp
from jax import lax
from jax.experimental import pallas as pl
from jax.experimental.pallas import tpu as pltpu
from jax.sharding import PartitionSpec as P

RATE = 0.5
THIN_LIMIT = 0.35
MESH = pl.DeviceIdType.MESH
F32 = jnp.float32
HIGHEST = lax.Precision.HIGHEST


def upwind(face, first, second):
    return jnp.maximum(face, 0.0) * first + jnp.minimum(face, 0.0) * second


def kernel(
    nb,
    nl,
    nbr_hbm,
    fold_hbm,
    side_hbm,
    t_hbm,
    u_hbm,
    v_hbm,
    w_hbm,
    g_hbm,
    bottom_hbm,
    shave_hbm,
    out_ref,
    t_ref,
    u_ref,
    v_ref,
    w_ref,
    g_ref,
    bottom_ref,
    shave_ref,
    nbr_ref,
    fold_ref,
    side_ref,
    x_ref,
    edge_ref,
    pay_ref,
    halo_ref,
    group_ref,
    parts_ref,
    in_sem,
    edge_send,
    edge_recv,
    group_send,
    group_recv,
    part_send,
    part_recv,
):
    levels, rows, cols = t_ref.shape
    n = nb * nl
    unroll = n <= 64
    block = lax.axis_index("blocks")
    lev = lax.axis_index("lev")

    def block_peers(visit):
        def step(i, carry):
            visit(i - 1, {"blocks": lax.rem(block + i, nb), "lev": lev})
            return carry

        lax.fori_loop(1, nb, step, 0, unroll=unroll)

    def lev_peers(visit):
        def step(i, carry):
            visit(i - 1, {"blocks": block, "lev": lax.rem(lev + i, nl)})
            return carry

        lax.fori_loop(1, nl, step, 0, unroll=unroll)

    loads = [
        pltpu.make_async_copy(src, dst, in_sem.at[i])
        for i, (src, dst) in enumerate(
            (
                (t_hbm, t_ref),
                (u_hbm, u_ref),
                (bottom_hbm, bottom_ref),
                (shave_hbm, shave_ref),
                (g_hbm, g_ref),
                (v_hbm, v_ref),
                (w_hbm, w_ref),
                (nbr_hbm, nbr_ref),
                (fold_hbm, fold_ref),
                (side_hbm, side_ref),
            )
        )
    ]
    for i in (7, 8, 9, 2, 3, 0, 1, 5, 4):
        loads[i].start()

    barrier = pltpu.get_barrier_semaphore()

    def greet(slot, device):
        pl.semaphore_signal(barrier, inc=1, device_id=device, device_id_type=MESH)

    block_peers(greet)
    lev_peers(greet)

    loads[6].start()

    lane = lax.broadcasted_iota(jnp.int32, (rows, cols), 1)
    row = lax.broadcasted_iota(jnp.int32, (rows, cols), 0)
    lane_pair = lane // 2

    for load in loads[:4]:
        load.wait()
    bottom = bottom_ref[...]
    shave = shave_ref[...]
    strip = jnp.zeros((rows, cols), F32)
    fields = [functools.partial(lambda k: t_ref[k], k) for k in range(levels)]
    fields += [functools.partial(lambda k: u_ref[k], k) for k in range(levels)]
    fields += [lambda: bottom.astype(F32), lambda: shave]
    for j, field in enumerate(fields):
        strip = jnp.where(lane_pair == j, pltpu.roll(field(), 2 * j + 1, 1), strip)
    edge_ref[...] = strip.T

    loads[5].wait()
    loads[7].wait()
    loads[8].wait()
    loads[9].wait()
    t_east = edge_ref[pl.ds(0, levels, stride=2), :]
    t_west = edge_ref[pl.ds(1, levels, stride=2), :]
    u_east = edge_ref[pl.ds(2 * levels, levels, stride=2), :]
    u_west = edge_ref[pl.ds(2 * levels + 1, levels, stride=2), :]
    t_south = t_ref[:, 0, :]
    t_north = t_ref[:, rows - 1, :]
    v_south = v_ref[:, 0, :]
    v_north = v_ref[:, rows - 1, :]
    t_edges = (t_west, t_east, t_south, t_north)
    f_edges = (u_west, u_east, v_south, v_north)
    sides = [nbr_ref[0, s] for s in range(4)]
    fold = fold_ref[0, 0]
    blank = jnp.zeros((levels, cols), F32)

    def compose(there):
        t_side, f_side = blank, blank
        for s in range(4):
            hit = sides[s] == there
            t_side = jnp.where(hit, t_edges[s], t_side)
            f_side = jnp.where(hit, f_edges[s], f_side)
        hit = fold == there
        return t_side, f_side, jnp.where(hit, t_north, blank), jnp.where(hit, v_north, blank)

    def pack(i, carry):
        parts = compose(lax.rem(block + i, nb))
        for p, part in enumerate(parts):
            pay_ref[i - 1, p * levels : (p + 1) * levels, :] = part
        return carry

    lax.fori_loop(1, nb, pack, 0, unroll=unroll)

    loads[4].wait()
    last = bottom - 1
    source = jnp.zeros((rows, cols), F32)
    for k in range(levels):
        thick = jnp.where(k < last, 1.0, jnp.where(k == last, shave, 0.0))
        source += thick * (RATE * (g_ref[k] - t_ref[k]))
    volume = jnp.where(bottom > 0, last.astype(F32) + shave, 0.0)
    source = jnp.sum(source, axis=0, keepdims=True)
    volume = jnp.sum(volume, axis=0, keepdims=True)
    half = cols // 2
    first_half = lax.broadcasted_iota(jnp.int32, (1, cols), 1) < half
    own_part = jnp.where(
        first_half,
        source + pltpu.roll(source, half, 1),
        volume + pltpu.roll(volume, half, 1),
    )
    group_ref[nb - 1] = own_part

    pl.semaphore_wait(barrier, nb + nl - 2)

    def send(src, dst, sems, device):
        pltpu.make_async_remote_copy(
            src_ref=src,
            dst_ref=dst,
            send_sem=sems[0],
            recv_sem=sems[1],
            device_id=device,
            device_id_type=MESH,
        ).start()

    block_peers(
        lambda slot, device: send(
            group_ref.at[nb - 1], group_ref.at[slot], (group_send, group_recv), device
        )
    )
    block_peers(
        lambda slot, device: send(
            pay_ref.at[slot], halo_ref.at[slot], (edge_send, edge_recv), device
        )
    )

    loads[6].wait()
    inverse = 1.0 / shave
    bottom_east = pltpu.roll(bottom, cols - 1, 1)
    open_east = jnp.where(lane == cols - 1, 0, jnp.minimum(bottom, bottom_east))
    open_north = jnp.where(row == rows - 1, 0, jnp.minimum(bottom, pltpu.roll(bottom, rows - 1, 0)))
    upper = jnp.zeros((rows, cols), F32)
    for k in range(levels):
        t = t_ref[k]
        u = u_ref[k]
        v = v_ref[k]
        face = jnp.where(k < open_east, 0.5 * (u + pltpu.roll(u, cols - 1, 1)), 0.0)
        flux = upwind(face, t, pltpu.roll(t, cols - 1, 1))
        divergence = pltpu.roll(flux, 1, 1) - flux
        face = jnp.where(k < open_north, 0.5 * (v + pltpu.roll(v, rows - 1, 0)), 0.0)
        flux = upwind(face, t, pltpu.roll(t, rows - 1, 0))
        divergence += pltpu.roll(flux, 1, 0) - flux
        if k < levels - 1:
            face = jnp.where(k + 1 < bottom, 0.5 * (w_ref[k] + w_ref[k + 1]), 0.0)
            lower = upwind(face, t_ref[k + 1], t)
        else:
            lower = jnp.zeros((rows, cols), F32)
        divergence += lower - upper
        upper = lower
        x_ref[k] = t + divergence * jnp.where(k == last, inverse, 1.0) + RATE * (g_ref[k] - t)

    received = group_ref.at[0 : nb - 1]
    pltpu.make_async_copy(received, received, group_recv).wait()
    lev_peers(
        lambda slot, device: send(group_ref, parts_ref.at[slot], (part_send, part_recv), device)
    )
    pltpu.make_async_copy(halo_ref, halo_ref, edge_recv).wait()

    own = compose(block)
    found_t = [jnp.where(sides[s] == block, t_edges[s ^ 1], blank) for s in range(4)]
    found_f = [jnp.where(sides[s] == block, f_edges[s ^ 1], blank) for s in range(4)]

    def collect(i, carry):
        found_t, found_f, fold_t, fold_f = carry
        origin = lax.rem(block + nb - i, nb)
        side_t, side_f, over_t, over_f = (
            halo_ref[i - 1, p * levels : (p + 1) * levels, :] for p in range(4)
        )
        found_t = [jnp.where(sides[s] == origin, side_t, found_t[s]) for s in range(4)]
        found_f = [jnp.where(sides[s] == origin, side_f, found_f[s]) for s in range(4)]
        hit = fold == origin
        return found_t, found_f, jnp.where(hit, over_t, fold_t), jnp.where(hit, over_f, fold_f)

    found_t, found_f, fold_t, fold_f = lax.fori_loop(
        1, nb, collect, (found_t, found_f, own[2], own[3]), unroll=unroll
    )
    mirror = (
        lax.broadcasted_iota(jnp.int32, (cols, cols), 0)
        + lax.broadcasted_iota(jnp.int32, (cols, cols), 1)
        == cols - 1
    ).astype(F32)
    turned = jnp.dot(
        jnp.concatenate([fold_t, fold_f], 0), mirror, precision=HIGHEST, preferred_element_type=F32
    )
    found_t[3] = found_t[3] + turned[:levels]
    found_f[3] = found_f[3] - turned[levels:]

    grid = lax.broadcasted_iota(jnp.int32, (levels, cols), 0).astype(F32)
    edge_bottom = (
        edge_ref[4 * levels + 1 : 4 * levels + 2, :],
        edge_ref[4 * levels : 4 * levels + 1, :],
        bottom_ref[0:1, :].astype(F32),
        bottom_ref[rows - 1 : rows, :].astype(F32),
    )
    edge_shave = (
        edge_ref[4 * levels + 3 : 4 * levels + 4, :],
        edge_ref[4 * levels + 2 : 4 * levels + 3, :],
        shave_ref[0:1, :],
        shave_ref[rows - 1 : rows, :],
    )
    gains = []
    for s in range(4):
        beyond = side_ref[s : s + 1, :].astype(F32)
        wet = grid < jnp.minimum(edge_bottom[s], beyond)
        face = jnp.where(wet, 0.5 * (f_edges[s] + found_f[s]), 0.0)
        if s % 2 == 0:
            flux = upwind(face, found_t[s], t_edges[s])
        else:
            flux = -upwind(face, t_edges[s], found_t[s])
        gains.append(flux * jnp.where(grid == edge_bottom[s] - 1.0, 1.0 / edge_shave[s], 1.0))
    for k in range(levels):
        x_ref[k, 0:1, :] += gains[2][k : k + 1, :]
        x_ref[k, rows - 1 : rows, :] += gains[3][k : k + 1, :]
    wide = jnp.concatenate(gains[:2], 0)
    place = lax.broadcasted_iota(jnp.int32, (2 * levels, cols), 0)
    place_lane = lax.broadcasted_iota(jnp.int32, (2 * levels, cols), 1)

    partner_shave = jnp.where(bottom_east == bottom, pltpu.roll(shave, cols - 1, 1), 1.0)
    scale = 1.0 / (shave + partner_shave)
    weight = shave * scale
    partner_weight = partner_shave * scale
    struck = jnp.where(shave < THIN_LIMIT, last, -1)
    struck_west = pltpu.roll(struck, 1, 1)

    for k in range(levels):
        chosen = (place == k) & (place_lane == 0) | (place == levels + k) & (place_lane == cols - 1)
        side_gain = lax.dot_general(
            wide,
            chosen.astype(F32),
            (((0,), (0,)), ((), ())),
            precision=HIGHEST,
            preferred_element_type=F32,
        )
        x = x_ref[k] + side_gain
        merged = weight * x + partner_weight * pltpu.roll(x, cols - 1, 1)
        x = jnp.where(struck == k, merged, x)
        x = jnp.where(struck_west == k, pltpu.roll(merged, 1, 1), x)
        x_ref[k] = x

    pltpu.make_async_copy(parts_ref, parts_ref, part_recv).wait()
    total = jnp.sum(group_ref[...], axis=0)
    total = lax.fori_loop(
        0, nl - 1, lambda i, carry: carry + jnp.sum(parts_ref[i], axis=0), total, unroll=unroll
    )
    total_source = jnp.sum(jnp.where(first_half, total, 0.0), axis=1, keepdims=True)
    total_volume = jnp.sum(jnp.where(first_half, 0.0, total), axis=1, keepdims=True)
    mean = total_source / total_volume

    for k in range(levels):
        out_ref[k] = jnp.where(k < bottom, x_ref[k] - mean, 0.0)

    pltpu.make_async_copy(halo_ref, halo_ref, edge_send).wait()
    pltpu.make_async_copy(received, received, group_send).wait()
    pltpu.make_async_copy(parts_ref, parts_ref, part_send).wait()


def local(
    nb,
    nl,
    tracers,
    east_velocity,
    north_velocity,
    upward_velocity,
    target,
    bottom,
    shave_fraction,
    side_bottom,
    neighbors,
    fold_partner,
    thin_pairs,
):
    levels, rows, cols = tracers.shape[2:]
    in_hbm = functools.partial(pltpu.with_memory_space_constraint, memory_space=pltpu.HBM)
    cube = (levels, rows, cols)
    n = nb * nl
    vmem = pl.BlockSpec(memory_space=pltpu.VMEM)
    grant = (12 << 20) + 4 * cols * (8 * levels * nb + 8 * n)
    anywhere = pl.BlockSpec(memory_space=pl.ANY)
    stepped = pl.pallas_call(
        functools.partial(kernel, nb, nl),
        out_shape=pltpu.VMEM(cube, F32),
        in_specs=[anywhere] * 10,
        out_specs=vmem,
        scratch_shapes=[
            pltpu.VMEM(cube, F32),
            pltpu.VMEM(cube, F32),
            pltpu.VMEM(cube, F32),
            pltpu.VMEM(cube, F32),
            pltpu.VMEM(cube, F32),
            pltpu.VMEM((rows, cols), jnp.int32),
            pltpu.VMEM((rows, cols), F32),
            pltpu.SMEM((1, 4), jnp.int32),
            pltpu.SMEM((1, 1), jnp.int32),
            pltpu.VMEM((4, cols), jnp.int32),
            pltpu.VMEM(cube, F32),
            pltpu.VMEM((cols, rows), F32),
            pltpu.VMEM((nb - 1, 4 * levels, cols), F32),
            pltpu.VMEM((nb - 1, 4 * levels, cols), F32),
            pltpu.VMEM((nb, 1, cols), F32),
            pltpu.VMEM((nl - 1, nb, 1, cols), F32),
            pltpu.SemaphoreType.DMA((10,)),
            pltpu.SemaphoreType.DMA,
            pltpu.SemaphoreType.DMA,
            pltpu.SemaphoreType.DMA,
            pltpu.SemaphoreType.DMA,
            pltpu.SemaphoreType.DMA,
            pltpu.SemaphoreType.DMA,
        ],
        compiler_params=pltpu.CompilerParams(
            collective_id=0, has_side_effects=True, vmem_limit_bytes=grant
        ),
    )(
        in_hbm(neighbors),
        fold_partner.reshape(1, 1),
        in_hbm(side_bottom.reshape(4, cols)),
        in_hbm(tracers.reshape(cube)),
        in_hbm(east_velocity.reshape(cube)),
        in_hbm(north_velocity.reshape(cube)),
        in_hbm(upward_velocity.reshape(cube)),
        in_hbm(target.reshape(cube)),
        in_hbm(bottom.reshape(rows, cols)),
        in_hbm(shave_fraction.reshape(rows, cols)),
    )
    return stepped.reshape(tracers.shape)


def solution(mesh):
    placed = (
        P("blocks", "lev", None, None, None),
        P("blocks", None, None, None),
        P("blocks", None, None, None),
        P("blocks", None, None, None),
        P("blocks", "lev", None, None, None),
        P("blocks", None, None),
        P("blocks", None, None),
        P("blocks", None, None),
        P("blocks", None),
        P("blocks"),
        P("blocks", None, None),
    )
    return jax.shard_map(
        functools.partial(local, mesh.shape["blocks"], mesh.shape["lev"]),
        mesh=mesh,
        in_specs=placed,
        out_specs=P("blocks", "lev", None, None, None),
        check_vma=False,
    )
```

```python
import functools

import jax
import jax.numpy as jnp
from jax import lax
from jax.experimental import pallas as pl
from jax.experimental.pallas import tpu as pltpu
from jax.sharding import PartitionSpec as P

RATE = 0.5
THIN_LIMIT = 0.35
MESH = pl.DeviceIdType.MESH
F32 = jnp.float32
HIGHEST = lax.Precision.HIGHEST


def upwind(face, first, second):
    return jnp.maximum(face, 0.0) * first + jnp.minimum(face, 0.0) * second


def kernel(
    nb,
    nl,
    nbr_hbm,
    fold_hbm,
    side_hbm,
    t_hbm,
    u_hbm,
    v_hbm,
    w_hbm,
    g_hbm,
    bottom_hbm,
    shave_hbm,
    out_ref,
    t_ref,
    u_ref,
    v_ref,
    w_ref,
    g_ref,
    bottom_ref,
    shave_ref,
    nbr_ref,
    fold_ref,
    side_ref,
    x_ref,
    edge_ref,
    pay_ref,
    halo_ref,
    part_ref,
    parts_ref,
    in_sem,
    edge_send,
    edge_recv,
    part_send,
    part_recv,
):
    levels, rows, cols = t_ref.shape
    n = nb * nl
    unroll = n <= 64
    block = lax.axis_index("blocks")
    lev = lax.axis_index("lev")

    def each_other(visit):
        def outer(i, carry):
            there = lax.rem(block + i, nb)

            def inner(j, carry):
                visit(i * nl + j - 1, {"blocks": there, "lev": lax.rem(lev + j, nl)})
                return carry

            return lax.fori_loop(0, nl, inner, carry, unroll=unroll)

        def first(j, carry):
            visit(j - 1, {"blocks": block, "lev": lax.rem(lev + j, nl)})
            return carry

        lax.fori_loop(1, nb, outer, 0, unroll=unroll)
        lax.fori_loop(1, nl, first, 0, unroll=unroll)

    loads = [
        pltpu.make_async_copy(src, dst, in_sem.at[i])
        for i, (src, dst) in enumerate(
            (
                (t_hbm, t_ref),
                (u_hbm, u_ref),
                (bottom_hbm, bottom_ref),
                (shave_hbm, shave_ref),
                (g_hbm, g_ref),
                (v_hbm.at[:, 8 : rows - 8, :], v_ref.at[:, 8 : rows - 8, :]),
                (w_hbm, w_ref),
                (nbr_hbm, nbr_ref),
                (fold_hbm, fold_ref),
                (side_hbm, side_ref),
                (v_hbm.at[:, 0:8, :], v_ref.at[:, 0:8, :]),
                (v_hbm.at[:, rows - 8 : rows, :], v_ref.at[:, rows - 8 : rows, :]),
            )
        )
    ]
    for i in (2, 3, 0, 4, 7, 8, 9, 10, 11, 1, 5, 6):
        loads[i].start()

    barrier = pltpu.get_barrier_semaphore()

    each_other(
        lambda slot, device: pl.semaphore_signal(
            barrier, inc=1, device_id=device, device_id_type=MESH
        )
    )

    lane = lax.broadcasted_iota(jnp.int32, (rows, cols), 1)
    row = lax.broadcasted_iota(jnp.int32, (rows, cols), 0)
    lane_pair = lane // 2

    for i in (2, 3, 0, 4):
        loads[i].wait()
    bottom = bottom_ref[...]
    shave = shave_ref[...]
    last = bottom - 1
    source = jnp.zeros((rows, cols), F32)
    for k in range(levels):
        thick = jnp.where(k < last, 1.0, jnp.where(k == last, shave, 0.0))
        source += thick * (RATE * (g_ref[k] - t_ref[k]))
    volume = jnp.where(bottom > 0, last.astype(F32) + shave, 0.0)
    source = jnp.sum(source, axis=0, keepdims=True)
    volume = jnp.sum(volume, axis=0, keepdims=True)
    half = cols // 2
    first_half = lax.broadcasted_iota(jnp.int32, (1, cols), 1) < half
    own_part = jnp.where(
        first_half,
        source + pltpu.roll(source, half, 1),
        volume + pltpu.roll(volume, half, 1),
    )
    part_ref[...] = own_part

    loads[1].wait()
    strip = jnp.zeros((rows, cols), F32)
    fields = [functools.partial(lambda k: t_ref[k], k) for k in range(levels)]
    fields += [functools.partial(lambda k: u_ref[k], k) for k in range(levels)]
    fields += [lambda: bottom.astype(F32), lambda: shave]
    for j, field in enumerate(fields):
        strip = jnp.where(lane_pair == j, pltpu.roll(field(), 2 * j + 1, 1), strip)
    edge_ref[...] = strip.T

    for i in (7, 8, 9, 10, 11):
        loads[i].wait()
    t_east = edge_ref[pl.ds(0, levels, stride=2), :]
    t_west = edge_ref[pl.ds(1, levels, stride=2), :]
    u_east = edge_ref[pl.ds(2 * levels, levels, stride=2), :]
    u_west = edge_ref[pl.ds(2 * levels + 1, levels, stride=2), :]
    t_south = t_ref[:, 0, :]
    t_north = t_ref[:, rows - 1, :]
    v_south = v_ref[:, 0, :]
    v_north = v_ref[:, rows - 1, :]
    t_edges = (t_west, t_east, t_south, t_north)
    f_edges = (u_west, u_east, v_south, v_north)
    sides = [nbr_ref[0, s] for s in range(4)]
    fold = fold_ref[0, 0]
    blank = jnp.zeros((levels, cols), F32)

    def compose(there):
        t_side, f_side = blank, blank
        for s in range(4):
            hit = sides[s] == there
            t_side = jnp.where(hit, t_edges[s], t_side)
            f_side = jnp.where(hit, f_edges[s], f_side)
        hit = fold == there
        return t_side, f_side, jnp.where(hit, t_north, blank), jnp.where(hit, v_north, blank)

    def pack(i, carry):
        parts = compose(lax.rem(block + i, nb))
        for p, part in enumerate(parts):
            pay_ref[i - 1, p * levels : (p + 1) * levels, :] = part
        return carry

    lax.fori_loop(1, nb, pack, 0, unroll=unroll)

    pl.semaphore_wait(barrier, n - 1)

    def send_edges(i, carry):
        pltpu.make_async_remote_copy(
            src_ref=pay_ref.at[i - 1],
            dst_ref=halo_ref.at[i - 1],
            send_sem=edge_send,
            recv_sem=edge_recv,
            device_id={"blocks": lax.rem(block + i, nb), "lev": lev},
            device_id_type=MESH,
        ).start()
        return carry

    each_other(
        lambda slot, device: pltpu.make_async_remote_copy(
            src_ref=part_ref,
            dst_ref=parts_ref.at[slot],
            send_sem=part_send,
            recv_sem=part_recv,
            device_id=device,
            device_id_type=MESH,
        ).start()
    )
    lax.fori_loop(1, nb, send_edges, 0, unroll=unroll)

    loads[5].wait()
    loads[6].wait()
    inverse = 1.0 / shave
    bottom_east = pltpu.roll(bottom, cols - 1, 1)
    open_east = jnp.where(lane == cols - 1, 0, jnp.minimum(bottom, bottom_east))
    open_north = jnp.where(row == rows - 1, 0, jnp.minimum(bottom, pltpu.roll(bottom, rows - 1, 0)))
    upper = jnp.zeros((rows, cols), F32)
    for k in range(levels):
        t = t_ref[k]
        u = u_ref[k]
        v = v_ref[k]
        face = jnp.where(k < open_east, 0.5 * (u + pltpu.roll(u, cols - 1, 1)), 0.0)
        flux = upwind(face, t, pltpu.roll(t, cols - 1, 1))
        divergence = pltpu.roll(flux, 1, 1) - flux
        face = jnp.where(k < open_north, 0.5 * (v + pltpu.roll(v, rows - 1, 0)), 0.0)
        flux = upwind(face, t, pltpu.roll(t, rows - 1, 0))
        divergence += pltpu.roll(flux, 1, 0) - flux
        if k < levels - 1:
            face = jnp.where(k + 1 < bottom, 0.5 * (w_ref[k] + w_ref[k + 1]), 0.0)
            lower = upwind(face, t_ref[k + 1], t)
        else:
            lower = jnp.zeros((rows, cols), F32)
        divergence += lower - upper
        upper = lower
        x_ref[k] = t + divergence * jnp.where(k == last, inverse, 1.0) + RATE * (g_ref[k] - t)

    pltpu.make_async_copy(halo_ref, halo_ref, edge_recv).wait()

    own = compose(block)
    found_t = [jnp.where(sides[s] == block, t_edges[s ^ 1], blank) for s in range(4)]
    found_f = [jnp.where(sides[s] == block, f_edges[s ^ 1], blank) for s in range(4)]

    def collect(i, carry):
        found_t, found_f, fold_t, fold_f = carry
        origin = lax.rem(block + nb - i, nb)
        side_t, side_f, over_t, over_f = (
            halo_ref[i - 1, p * levels : (p + 1) * levels, :] for p in range(4)
        )
        found_t = [jnp.where(sides[s] == origin, side_t, found_t[s]) for s in range(4)]
        found_f = [jnp.where(sides[s] == origin, side_f, found_f[s]) for s in range(4)]
        hit = fold == origin
        return found_t, found_f, jnp.where(hit, over_t, fold_t), jnp.where(hit, over_f, fold_f)

    found_t, found_f, fold_t, fold_f = lax.fori_loop(
        1, nb, collect, (found_t, found_f, own[2], own[3]), unroll=unroll
    )
    mirror = (
        lax.broadcasted_iota(jnp.int32, (cols, cols), 0)
        + lax.broadcasted_iota(jnp.int32, (cols, cols), 1)
        == cols - 1
    ).astype(F32)
    turned = jnp.dot(
        jnp.concatenate([fold_t, fold_f], 0), mirror, precision=HIGHEST, preferred_element_type=F32
    )
    found_t[3] = found_t[3] + turned[:levels]
    found_f[3] = found_f[3] - turned[levels:]

    grid = lax.broadcasted_iota(jnp.int32, (levels, cols), 0).astype(F32)
    edge_bottom = (
        edge_ref[4 * levels + 1 : 4 * levels + 2, :],
        edge_ref[4 * levels : 4 * levels + 1, :],
        bottom_ref[0:1, :].astype(F32),
        bottom_ref[rows - 1 : rows, :].astype(F32),
    )
    edge_shave = (
        edge_ref[4 * levels + 3 : 4 * levels + 4, :],
        edge_ref[4 * levels + 2 : 4 * levels + 3, :],
        shave_ref[0:1, :],
        shave_ref[rows - 1 : rows, :],
    )
    gains = []
    for s in range(4):
        beyond = side_ref[s : s + 1, :].astype(F32)
        wet = grid < jnp.minimum(edge_bottom[s], beyond)
        face = jnp.where(wet, 0.5 * (f_edges[s] + found_f[s]), 0.0)
        if s % 2 == 0:
            flux = upwind(face, found_t[s], t_edges[s])
        else:
            flux = -upwind(face, t_edges[s], found_t[s])
        gains.append(flux * jnp.where(grid == edge_bottom[s] - 1.0, 1.0 / edge_shave[s], 1.0))
    for k in range(levels):
        x_ref[k, 0:1, :] += gains[2][k : k + 1, :]
        x_ref[k, rows - 1 : rows, :] += gains[3][k : k + 1, :]
    wide = jnp.concatenate(gains[:2], 0)
    place = lax.broadcasted_iota(jnp.int32, (2 * levels, cols), 0)
    place_lane = lax.broadcasted_iota(jnp.int32, (2 * levels, cols), 1)

    partner_shave = jnp.where(bottom_east == bottom, pltpu.roll(shave, cols - 1, 1), 1.0)
    scale = 1.0 / (shave + partner_shave)
    weight = shave * scale
    partner_weight = partner_shave * scale
    struck = jnp.where(shave < THIN_LIMIT, last, -1)
    struck_west = pltpu.roll(struck, 1, 1)

    for k in range(levels):
        chosen = (place == k) & (place_lane == 0) | (place == levels + k) & (place_lane == cols - 1)
        side_gain = lax.dot_general(
            wide,
            chosen.astype(F32),
            (((0,), (0,)), ((), ())),
            precision=HIGHEST,
            preferred_element_type=F32,
        )
        x = x_ref[k] + side_gain
        merged = weight * x + partner_weight * pltpu.roll(x, cols - 1, 1)
        x = jnp.where(struck == k, merged, x)
        x = jnp.where(struck_west == k, pltpu.roll(merged, 1, 1), x)
        x_ref[k] = x

    pltpu.make_async_copy(parts_ref, parts_ref, part_recv).wait()
    total = lax.fori_loop(
        0, n - 1, lambda i, carry: carry + parts_ref[i], own_part, unroll=unroll
    )
    total_source = jnp.sum(jnp.where(first_half, total, 0.0), axis=1, keepdims=True)
    total_volume = jnp.sum(jnp.where(first_half, 0.0, total), axis=1, keepdims=True)
    mean = total_source / total_volume

    for k in range(levels):
        out_ref[k] = jnp.where(k < bottom, x_ref[k] - mean, 0.0)

    pltpu.make_async_copy(halo_ref, halo_ref, edge_send).wait()
    pltpu.make_async_copy(parts_ref, parts_ref, part_send).wait()


def local(
    nb,
    nl,
    tracers,
    east_velocity,
    north_velocity,
    upward_velocity,
    target,
    bottom,
    shave_fraction,
    side_bottom,
    neighbors,
    fold_partner,
    thin_pairs,
):
    levels, rows, cols = tracers.shape[2:]
    in_hbm = functools.partial(pltpu.with_memory_space_constraint, memory_space=pltpu.HBM)
    cube = (levels, rows, cols)
    n = nb * nl
    vmem = pl.BlockSpec(memory_space=pltpu.VMEM)
    grant = (12 << 20) + 4 * cols * (8 * levels * nb + 8 * n)
    anywhere = pl.BlockSpec(memory_space=pl.ANY)
    stepped = pl.pallas_call(
        functools.partial(kernel, nb, nl),
        out_shape=pltpu.VMEM(cube, F32),
        in_specs=[anywhere] * 10,
        out_specs=vmem,
        scratch_shapes=[
            pltpu.VMEM(cube, F32),
            pltpu.VMEM(cube, F32),
            pltpu.VMEM(cube, F32),
            pltpu.VMEM(cube, F32),
            pltpu.VMEM(cube, F32),
            pltpu.VMEM((rows, cols), jnp.int32),
            pltpu.VMEM((rows, cols), F32),
            pltpu.SMEM((1, 4), jnp.int32),
            pltpu.SMEM((1, 1), jnp.int32),
            pltpu.VMEM((4, cols), jnp.int32),
            pltpu.VMEM(cube, F32),
            pltpu.VMEM((cols, rows), F32),
            pltpu.VMEM((nb - 1, 4 * levels, cols), F32),
            pltpu.VMEM((nb - 1, 4 * levels, cols), F32),
            pltpu.VMEM((1, cols), F32),
            pltpu.VMEM((n - 1, 1, cols), F32),
            pltpu.SemaphoreType.DMA((12,)),
            pltpu.SemaphoreType.DMA,
            pltpu.SemaphoreType.DMA,
            pltpu.SemaphoreType.DMA,
            pltpu.SemaphoreType.DMA,
        ],
        compiler_params=pltpu.CompilerParams(
            collective_id=0, has_side_effects=True, vmem_limit_bytes=grant
        ),
    )(
        in_hbm(neighbors),
        fold_partner.reshape(1, 1),
        in_hbm(side_bottom.reshape(4, cols)),
        in_hbm(tracers.reshape(cube)),
        in_hbm(east_velocity.reshape(cube)),
        in_hbm(north_velocity.reshape(cube)),
        in_hbm(upward_velocity.reshape(cube)),
        in_hbm(target.reshape(cube)),
        in_hbm(bottom.reshape(rows, cols)),
        in_hbm(shave_fraction.reshape(rows, cols)),
    )
    return stepped.reshape(tracers.shape)


def solution(mesh):
    placed = (
        P("blocks", "lev", None, None, None),
        P("blocks", None, None, None),
        P("blocks", None, None, None),
        P("blocks", None, None, None),
        P("blocks", "lev", None, None, None),
        P("blocks", None, None),
        P("blocks", None, None),
        P("blocks", None, None),
        P("blocks", None),
        P("blocks"),
        P("blocks", None, None),
    )
    return jax.shard_map(
        functools.partial(local, mesh.shape["blocks"], mesh.shape["lev"]),
        mesh=mesh,
        in_specs=placed,
        out_specs=P("blocks", "lev", None, None, None),
        check_vma=False,
    )
```

```python
import functools

import jax
import jax.numpy as jnp
from jax import lax
from jax.experimental import pallas as pl
from jax.experimental.pallas import tpu as pltpu
from jax.sharding import PartitionSpec as P

RATE = 0.5
THIN_LIMIT = 0.35
MESH = pl.DeviceIdType.MESH
F32 = jnp.float32
HIGHEST = lax.Precision.HIGHEST


def upwind(face, first, second):
    return jnp.maximum(face, 0.0) * first + jnp.minimum(face, 0.0) * second


def kernel(
    nb,
    nl,
    nbr_hbm,
    fold_hbm,
    side_hbm,
    t_hbm,
    u_hbm,
    v_hbm,
    w_hbm,
    g_hbm,
    bottom_hbm,
    shave_hbm,
    out_ref,
    t_ref,
    u_ref,
    v_ref,
    w_ref,
    g_ref,
    bottom_ref,
    shave_ref,
    nbr_ref,
    fold_ref,
    side_ref,
    x_ref,
    edge_ref,
    pay_ref,
    halo_ref,
    part_ref,
    parts_ref,
    in_sem,
    edge_send,
    edge_recv,
    part_send,
    part_recv,
):
    levels, rows, cols = t_ref.shape
    n = nb * nl
    unroll = n <= 64
    block = lax.axis_index("blocks")
    lev = lax.axis_index("lev")

    def each_other(visit):
        def outer(i, carry):
            there = lax.rem(block + i, nb)

            def inner(j, carry):
                visit(i * nl + j - 1, {"blocks": there, "lev": lax.rem(lev + j, nl)})
                return carry

            return lax.fori_loop(0, nl, inner, carry, unroll=unroll)

        def first(j, carry):
            visit(j - 1, {"blocks": block, "lev": lax.rem(lev + j, nl)})
            return carry

        lax.fori_loop(1, nb, outer, 0, unroll=unroll)
        lax.fori_loop(1, nl, first, 0, unroll=unroll)

    loads = [
        pltpu.make_async_copy(src, dst, in_sem.at[i])
        for i, (src, dst) in enumerate(
            (
                (t_hbm, t_ref),
                (u_hbm, u_ref),
                (bottom_hbm, bottom_ref),
                (shave_hbm, shave_ref),
                (g_hbm, g_ref),
                (v_hbm.at[:, 8 : rows - 8, :], v_ref.at[:, 8 : rows - 8, :]),
                (w_hbm, w_ref),
                (nbr_hbm, nbr_ref),
                (fold_hbm, fold_ref),
                (side_hbm, side_ref),
                (v_hbm.at[:, 0:8, :], v_ref.at[:, 0:8, :]),
                (v_hbm.at[:, rows - 8 : rows, :], v_ref.at[:, rows - 8 : rows, :]),
            )
        )
    ]
    for i in (2, 3, 0, 4, 7, 8, 9, 10, 11, 1, 5, 6):
        loads[i].start()

    barrier = pltpu.get_barrier_semaphore()

    each_other(
        lambda slot, device: pl.semaphore_signal(
            barrier, inc=1, device_id=device, device_id_type=MESH
        )
    )

    lane = lax.broadcasted_iota(jnp.int32, (rows, cols), 1)
    row = lax.broadcasted_iota(jnp.int32, (rows, cols), 0)
    lane_pair = lane // 2

    for i in (2, 3, 0, 4):
        loads[i].wait()
    bottom = bottom_ref[...]
    shave = shave_ref[...]
    last = bottom - 1
    source = jnp.zeros((rows, cols), F32)
    for k in range(levels):
        thick = jnp.where(k < last, 1.0, jnp.where(k == last, shave, 0.0))
        source += thick * (RATE * (g_ref[k] - t_ref[k]))
    volume = jnp.where(bottom > 0, last.astype(F32) + shave, 0.0)
    source = jnp.sum(source, axis=0, keepdims=True)
    volume = jnp.sum(volume, axis=0, keepdims=True)
    half = cols // 2
    first_half = lax.broadcasted_iota(jnp.int32, (1, cols), 1) < half
    own_part = jnp.where(
        first_half,
        source + pltpu.roll(source, half, 1),
        volume + pltpu.roll(volume, half, 1),
    )
    part_ref[...] = own_part

    loads[1].wait()
    strip = jnp.zeros((rows, cols), F32)
    fields = [functools.partial(lambda k: t_ref[k], k) for k in range(levels)]
    fields += [functools.partial(lambda k: u_ref[k], k) for k in range(levels)]
    fields += [lambda: bottom.astype(F32), lambda: shave]
    for j, field in enumerate(fields):
        strip = jnp.where(lane_pair == j, pltpu.roll(field(), 2 * j + 1, 1), strip)
    edge_ref[...] = strip.T

    for i in (7, 8, 9, 10, 11):
        loads[i].wait()
    t_east = edge_ref[pl.ds(0, levels, stride=2), :]
    t_west = edge_ref[pl.ds(1, levels, stride=2), :]
    u_east = edge_ref[pl.ds(2 * levels, levels, stride=2), :]
    u_west = edge_ref[pl.ds(2 * levels + 1, levels, stride=2), :]
    t_south = t_ref[:, 0, :]
    t_north = t_ref[:, rows - 1, :]
    v_south = v_ref[:, 0, :]
    v_north = v_ref[:, rows - 1, :]
    t_edges = (t_west, t_east, t_south, t_north)
    f_edges = (u_west, u_east, v_south, v_north)
    sides = [nbr_ref[0, s] for s in range(4)]
    fold = fold_ref[0, 0]
    blank = jnp.zeros((levels, cols), F32)

    def compose(there):
        t_side, f_side = blank, blank
        for s in range(4):
            hit = sides[s] == there
            t_side = jnp.where(hit, t_edges[s], t_side)
            f_side = jnp.where(hit, f_edges[s], f_side)
        hit = fold == there
        return t_side, f_side, jnp.where(hit, t_north, blank), jnp.where(hit, v_north, blank)

    def pack(i, carry):
        parts = compose(lax.rem(block + i, nb))
        for p, part in enumerate(parts):
            pay_ref[i - 1, p * levels : (p + 1) * levels, :] = part
        return carry

    lax.fori_loop(1, nb, pack, 0, unroll=unroll)

    pl.semaphore_wait(barrier, n - 1)

    def send_edges(i, carry):
        pltpu.make_async_remote_copy(
            src_ref=pay_ref.at[i - 1],
            dst_ref=halo_ref.at[i - 1],
            send_sem=edge_send,
            recv_sem=edge_recv,
            device_id={"blocks": lax.rem(block + i, nb), "lev": lev},
            device_id_type=MESH,
        ).start()
        return carry

    lax.fori_loop(1, nb, send_edges, 0, unroll=unroll)
    each_other(
        lambda slot, device: pltpu.make_async_remote_copy(
            src_ref=part_ref,
            dst_ref=parts_ref.at[slot],
            send_sem=part_send,
            recv_sem=part_recv,
            device_id=device,
            device_id_type=MESH,
        ).start()
    )

    loads[5].wait()
    loads[6].wait()
    inverse = 1.0 / shave
    bottom_east = pltpu.roll(bottom, cols - 1, 1)
    open_east = jnp.where(lane == cols - 1, 0, jnp.minimum(bottom, bottom_east))
    open_north = jnp.where(row == rows - 1, 0, jnp.minimum(bottom, pltpu.roll(bottom, rows - 1, 0)))
    upper = jnp.zeros((rows, cols), F32)
    for k in range(levels):
        t = t_ref[k]
        u = u_ref[k]
        v = v_ref[k]
        face = jnp.where(k < open_east, 0.5 * (u + pltpu.roll(u, cols - 1, 1)), 0.0)
        flux = upwind(face, t, pltpu.roll(t, cols - 1, 1))
        divergence = pltpu.roll(flux, 1, 1) - flux
        face = jnp.where(k < open_north, 0.5 * (v + pltpu.roll(v, rows - 1, 0)), 0.0)
        flux = upwind(face, t, pltpu.roll(t, rows - 1, 0))
        divergence += pltpu.roll(flux, 1, 0) - flux
        if k < levels - 1:
            face = jnp.where(k + 1 < bottom, 0.5 * (w_ref[k] + w_ref[k + 1]), 0.0)
            lower = upwind(face, t_ref[k + 1], t)
        else:
            lower = jnp.zeros((rows, cols), F32)
        divergence += lower - upper
        upper = lower
        x_ref[k] = t + divergence * jnp.where(k == last, inverse, 1.0) + RATE * (g_ref[k] - t)

    pltpu.make_async_copy(halo_ref, halo_ref, edge_recv).wait()

    own = compose(block)
    found_t = [jnp.where(sides[s] == block, t_edges[s ^ 1], blank) for s in range(4)]
    found_f = [jnp.where(sides[s] == block, f_edges[s ^ 1], blank) for s in range(4)]

    def collect(i, carry):
        found_t, found_f, fold_t, fold_f = carry
        origin = lax.rem(block + nb - i, nb)
        side_t, side_f, over_t, over_f = (
            halo_ref[i - 1, p * levels : (p + 1) * levels, :] for p in range(4)
        )
        found_t = [jnp.where(sides[s] == origin, side_t, found_t[s]) for s in range(4)]
        found_f = [jnp.where(sides[s] == origin, side_f, found_f[s]) for s in range(4)]
        hit = fold == origin
        return found_t, found_f, jnp.where(hit, over_t, fold_t), jnp.where(hit, over_f, fold_f)

    found_t, found_f, fold_t, fold_f = lax.fori_loop(
        1, nb, collect, (found_t, found_f, own[2], own[3]), unroll=unroll
    )
    mirror = (
        lax.broadcasted_iota(jnp.int32, (cols, cols), 0)
        + lax.broadcasted_iota(jnp.int32, (cols, cols), 1)
        == cols - 1
    ).astype(F32)
    turned = jnp.dot(
        jnp.concatenate([fold_t, fold_f], 0), mirror, precision=HIGHEST, preferred_element_type=F32
    )
    found_t[3] = found_t[3] + turned[:levels]
    found_f[3] = found_f[3] - turned[levels:]

    grid = lax.broadcasted_iota(jnp.int32, (levels, cols), 0).astype(F32)
    edge_bottom = (
        edge_ref[4 * levels + 1 : 4 * levels + 2, :],
        edge_ref[4 * levels : 4 * levels + 1, :],
        bottom_ref[0:1, :].astype(F32),
        bottom_ref[rows - 1 : rows, :].astype(F32),
    )
    edge_shave = (
        edge_ref[4 * levels + 3 : 4 * levels + 4, :],
        edge_ref[4 * levels + 2 : 4 * levels + 3, :],
        shave_ref[0:1, :],
        shave_ref[rows - 1 : rows, :],
    )
    gains = []
    for s in range(4):
        beyond = side_ref[s : s + 1, :].astype(F32)
        wet = grid < jnp.minimum(edge_bottom[s], beyond)
        face = jnp.where(wet, 0.5 * (f_edges[s] + found_f[s]), 0.0)
        if s % 2 == 0:
            flux = upwind(face, found_t[s], t_edges[s])
        else:
            flux = -upwind(face, t_edges[s], found_t[s])
        gains.append(flux * jnp.where(grid == edge_bottom[s] - 1.0, 1.0 / edge_shave[s], 1.0))
    for k in range(levels):
        x_ref[k, 0:1, :] += gains[2][k : k + 1, :]
        x_ref[k, rows - 1 : rows, :] += gains[3][k : k + 1, :]
    wide = jnp.concatenate(gains[:2], 0)
    place = lax.broadcasted_iota(jnp.int32, (2 * levels, cols), 0)
    place_lane = lax.broadcasted_iota(jnp.int32, (2 * levels, cols), 1)

    partner_shave = jnp.where(bottom_east == bottom, pltpu.roll(shave, cols - 1, 1), 1.0)
    scale = 1.0 / (shave + partner_shave)
    weight = shave * scale
    partner_weight = partner_shave * scale
    struck = jnp.where(shave < THIN_LIMIT, last, -1)
    struck_west = pltpu.roll(struck, 1, 1)

    for k in range(levels):
        chosen = (place == k) & (place_lane == 0) | (place == levels + k) & (place_lane == cols - 1)
        side_gain = lax.dot_general(
            wide,
            chosen.astype(F32),
            (((0,), (0,)), ((), ())),
            precision=HIGHEST,
            preferred_element_type=F32,
        )
        x = x_ref[k] + side_gain
        merged = weight * x + partner_weight * pltpu.roll(x, cols - 1, 1)
        x = jnp.where(struck == k, merged, x)
        x = jnp.where(struck_west == k, pltpu.roll(merged, 1, 1), x)
        x_ref[k] = x

    pltpu.make_async_copy(parts_ref, parts_ref, part_recv).wait()
    total = lax.fori_loop(
        0, n - 1, lambda i, carry: carry + parts_ref[i], own_part, unroll=unroll
    )
    total_source = jnp.sum(jnp.where(first_half, total, 0.0), axis=1, keepdims=True)
    total_volume = jnp.sum(jnp.where(first_half, 0.0, total), axis=1, keepdims=True)
    mean = total_source / total_volume

    for k in range(levels):
        out_ref[k] = jnp.where(k < bottom, x_ref[k] - mean, 0.0)

    pltpu.make_async_copy(halo_ref, halo_ref, edge_send).wait()
    pltpu.make_async_copy(parts_ref, parts_ref, part_send).wait()


def local(
    nb,
    nl,
    tracers,
    east_velocity,
    north_velocity,
    upward_velocity,
    target,
    bottom,
    shave_fraction,
    side_bottom,
    neighbors,
    fold_partner,
    thin_pairs,
):
    levels, rows, cols = tracers.shape[2:]
    in_hbm = functools.partial(pltpu.with_memory_space_constraint, memory_space=pltpu.HBM)
    cube = (levels, rows, cols)
    n = nb * nl
    vmem = pl.BlockSpec(memory_space=pltpu.VMEM)
    grant = (12 << 20) + 4 * cols * (8 * levels * nb + 8 * n)
    anywhere = pl.BlockSpec(memory_space=pl.ANY)
    stepped = pl.pallas_call(
        functools.partial(kernel, nb, nl),
        out_shape=pltpu.VMEM(cube, F32),
        in_specs=[anywhere] * 10,
        out_specs=vmem,
        scratch_shapes=[
            pltpu.VMEM(cube, F32),
            pltpu.VMEM(cube, F32),
            pltpu.VMEM(cube, F32),
            pltpu.VMEM(cube, F32),
            pltpu.VMEM(cube, F32),
            pltpu.VMEM((rows, cols), jnp.int32),
            pltpu.VMEM((rows, cols), F32),
            pltpu.SMEM((1, 4), jnp.int32),
            pltpu.SMEM((1, 1), jnp.int32),
            pltpu.VMEM((4, cols), jnp.int32),
            pltpu.VMEM(cube, F32),
            pltpu.VMEM((cols, rows), F32),
            pltpu.VMEM((nb - 1, 4 * levels, cols), F32),
            pltpu.VMEM((nb - 1, 4 * levels, cols), F32),
            pltpu.VMEM((1, cols), F32),
            pltpu.VMEM((n - 1, 1, cols), F32),
            pltpu.SemaphoreType.DMA((12,)),
            pltpu.SemaphoreType.DMA,
            pltpu.SemaphoreType.DMA,
            pltpu.SemaphoreType.DMA,
            pltpu.SemaphoreType.DMA,
        ],
        compiler_params=pltpu.CompilerParams(
            collective_id=0, has_side_effects=True, vmem_limit_bytes=grant
        ),
    )(
        in_hbm(neighbors),
        fold_partner.reshape(1, 1),
        in_hbm(side_bottom.reshape(4, cols)),
        in_hbm(tracers.reshape(cube)),
        in_hbm(east_velocity.reshape(cube)),
        in_hbm(north_velocity.reshape(cube)),
        in_hbm(upward_velocity.reshape(cube)),
        in_hbm(target.reshape(cube)),
        in_hbm(bottom.reshape(rows, cols)),
        in_hbm(shave_fraction.reshape(rows, cols)),
    )
    return stepped.reshape(tracers.shape)


def solution(mesh):
    placed = (
        P("blocks", "lev", None, None, None),
        P("blocks", None, None, None),
        P("blocks", None, None, None),
        P("blocks", None, None, None),
        P("blocks", "lev", None, None, None),
        P("blocks", None, None),
        P("blocks", None, None),
        P("blocks", None, None),
        P("blocks", None),
        P("blocks"),
        P("blocks", None, None),
    )
    return jax.shard_map(
        functools.partial(local, mesh.shape["blocks"], mesh.shape["lev"]),
        mesh=mesh,
        in_specs=placed,
        out_specs=P("blocks", "lev", None, None, None),
        check_vma=False,
    )
```
